256 devices in a mesh: dp: 4 (over z_lo, core), seq: 64 (over z_hi, y, x).
Axes of the slice: x: 4, y: 4, z: 8 (z_hi: 4, z_lo: 2; z = z_hi * 2 + z_lo), core: 2. Of those that a mesh axis runs over, the one named last changes fastest.
Arguments:
- tokens: bfloat16 [4, 128, 524288], P('dp', None, 'seq'), may hold values from -6 to 6
- kernel: bfloat16 [2, 128, 524288], P(None, None, 'seq'), may hold values from -6 to 6
- skip: float32 [128], replicated, may hold values from -4 to 4
- w_proj: bfloat16 [128, 256], replicated, may hold values from -0.5 to 0.5
- w_out: bfloat16 [128, 128], replicated, may hold values from -0.5 to 0.5
- cotangent: bfloat16 [4, 128, 524288], P('dp', None, 'seq'), may hold values from -6 to 6
Outputs:
- input_grad: bfloat16 [4, 128, 524288], P('dp', None, 'seq')
- kernel_grad: bfloat16 [2, 128, 524288], P(None, 'dp', 'seq')
The draws below stay inside these ranges and needn't reach their ends.
All inputs are finite; a program needn't handle non-finite values.
Results may differ from the reference program's by a relative error of at most 0.013.
Values may be sent and summed in bfloat16 or wider, within the bound.
No kernel may reach another device: no remote copies, remote signals or barrier semaphores. Data moves between devices by JAX's collectives and lax.ppermute only.
A program may use at most 128 MiB of HBM per device.

```python
import math
import jax
import jax.numpy as jnp
from jax import lax

C = 128
F2 = 64
F3 = 128
F1 = 64
NLEN = 524288
SEQS = 4


def block_levels(key, dims, shards, least, top_value):
    level = 1.0
    for axis_at, shards_of in shards:
        heights = jax.random.uniform(jax.random.fold_in(jax.random.fold_in(key, 6), axis_at), (shards_of,), jnp.float32, least / len(shards), top_value / len(shards))
        level = level * jnp.repeat(jnp.exp(heights), dims[axis_at] // shards_of).reshape((-1,) + (1,) * (len(dims) - 1 - axis_at))
    return level


def bell_draw(own_key, extent, scale, bound, pieces=(), kind=jnp.bfloat16):
    loudness = block_levels(own_key, extent, pieces, -0.22, 0.18) if pieces else 1.0
    drawn = jax.random.normal(own_key, extent, jnp.float32) * scale * loudness
    return jnp.minimum(jnp.maximum(drawn, -bound), bound).astype(kind)


def setup_inputs(seed: int = 0) -> dict:
    arg_keys = jax.random.split(jax.random.key(seed), 7)
    return {
        "tokens": bell_draw(arg_keys[0], (SEQS, C, NLEN), 1.0, 6.0, ((0, 4), (2, 64))),
        "kernel": bell_draw(arg_keys[1], (2, C, NLEN), 1.0, 6.0, ((2, 64),)),
        "skip": bell_draw(arg_keys[2], (C,), 1.0, 4.0, (), jnp.float32),
        "w_proj": bell_draw(arg_keys[3], (C, 2 * C), C ** -0.5, 0.5),
        "w_out": bell_draw(arg_keys[4], (C, C), C ** -0.5, 0.5),
        "cotangent": bell_draw(arg_keys[5], (SEQS, C, NLEN), 1.0, 6.0, ((0, 4), (2, 64))),
    }


def dft_pair(length, direction):
    indices = jnp.arange(length, dtype=jnp.int32)
    turn_ids = indices[:, None] * indices[None, :] % length
    angles = turn_ids.astype(jnp.float32) * (2.0 * math.pi / length)
    factor = 1.0 / math.sqrt(length)
    real_part = (jnp.cos(angles) * factor).astype(jnp.bfloat16)
    imag_part = (direction * jnp.sin(angles) * factor).astype(jnp.bfloat16)
    return (real_part, imag_part)

def block_matrix(length, direction):
    real_part, imag_part = dft_pair(length, direction)
    top_row = jnp.stack([real_part, -imag_part], axis=1)
    bottom_row = jnp.stack([imag_part, real_part], axis=1)
    return jnp.stack([top_row, bottom_row], axis=0).astype(jnp.float32)

def twiddle(turn_ids, modulus, direction):
    angles = (turn_ids % modulus).astype(jnp.float32) * (2.0 * math.pi / modulus)
    return (jnp.cos(angles), direction * jnp.sin(angles))

def rotate(stacked, cos_part, sin_part):
    real_out = stacked[0] * cos_part - stacked[1] * sin_part
    imag_out = stacked[0] * sin_part + stacked[1] * cos_part
    return jnp.stack([real_out, imag_out]).astype(jnp.bfloat16)

def complex_product(spectrum_a, spectrum_b, conjugate_first):
    a_real = spectrum_a[0].astype(jnp.float32)
    a_imag = spectrum_a[1].astype(jnp.float32)
    if conjugate_first:
        a_imag = -a_imag
    b_real = spectrum_b[0].astype(jnp.float32)
    b_imag = spectrum_b[1].astype(jnp.float32)
    return jnp.stack([a_real * b_real - a_imag * b_imag, a_real * b_imag + a_imag * b_real])

def position_grid():
    return jnp.arange(F2, dtype=jnp.int32)[:, None] * F3 + jnp.arange(F3, dtype=jnp.int32)[None, :]

def forward_ref(signal):
    real_part, imag_part = dft_pair(F1, -1.0)
    matrix = jnp.stack([real_part, imag_part]).astype(jnp.float32)
    combined = jnp.einsum('okn,cnqt->ockqt', matrix, signal.astype(jnp.float32))
    frequency = jnp.arange(F1, dtype=jnp.int32)[:, None, None]
    cos_part, sin_part = twiddle(frequency * position_grid()[None], NLEN, -1.0)
    section_one = rotate(combined, cos_part, sin_part)
    combined = jnp.einsum('opiq,ickqt->ockpt', block_matrix(F2, -1.0), section_one.astype(jnp.float32))
    cos_two, sin_two = twiddle(jnp.arange(F2, dtype=jnp.int32)[:, None] * jnp.arange(F3, dtype=jnp.int32)[None, :], F2 * F3, -1.0)
    section_two = rotate(combined, cos_two, sin_two)
    return jnp.einsum('opiq,ickjq->ockjp', block_matrix(F3, -1.0), section_two.astype(jnp.float32)).astype(jnp.bfloat16)

def inverse_ref(spectrum):
    combined = jnp.einsum('opiq,ickjq->ockjp', block_matrix(F3, 1.0), spectrum.astype(jnp.float32))
    cos_two, sin_two = twiddle(jnp.arange(F2, dtype=jnp.int32)[:, None] * jnp.arange(F3, dtype=jnp.int32)[None, :], F2 * F3, 1.0)
    back_one = rotate(combined, cos_two, sin_two)
    combined = jnp.einsum('opiq,ickqt->ockpt', block_matrix(F2, 1.0), back_one.astype(jnp.float32))
    frequency = jnp.arange(F1, dtype=jnp.int32)[:, None, None]
    cos_part, sin_part = twiddle(frequency * position_grid()[None], NLEN, 1.0)
    back_two = rotate(combined, cos_part, sin_part)
    real_part, imag_part = dft_pair(F1, 1.0)
    matrix = jnp.stack([real_part, -imag_part]).astype(jnp.float32)
    return jnp.einsum('ink,ickqt->cnqt', matrix, back_two.astype(jnp.float32)).astype(jnp.bfloat16)

def reference(tokens, kernel, skip, w_proj, w_out, cotangent):
    kernel_local = kernel.reshape(2, C, F1, F2, F3)
    skip_col = skip[:, None, None, None]

    def one_sequence(running, inputs):
        signal = inputs[0].reshape(C, F1, F2, F3)
        grad_in = inputs[1].reshape(C, F1, F2, F3)
        projected = jnp.einsum('ce,cnqt->enqt', w_proj.astype(jnp.float32), signal.astype(jnp.float32))
        values = projected[:C].astype(jnp.bfloat16)
        gates = projected[C:]
        spec_values = forward_ref(values)
        product = complex_product(kernel_local, spec_values, False).astype(jnp.bfloat16)
        convolved = inverse_ref(product)
        mixed = convolved.astype(jnp.float32) + skip_col * values.astype(jnp.float32)
        grad_hidden = jnp.einsum('cd,dnqt->cnqt', w_out.astype(jnp.float32), grad_in.astype(jnp.float32))
        grad_mixed = (grad_hidden * gates).astype(jnp.bfloat16)
        grad_gates = grad_hidden * mixed
        spec_grad = forward_ref(grad_mixed)
        kernel_terms = complex_product(spec_values, spec_grad, True).astype(jnp.bfloat16)
        kernel_terms = lax.optimization_barrier(kernel_terms).astype(jnp.float32)
        back_product = complex_product(kernel_local, spec_grad, True).astype(jnp.bfloat16)
        back_conv = inverse_ref(back_product)
        grad_values = back_conv.astype(jnp.float32) + skip_col * grad_mixed.astype(jnp.float32)
        grad_proj = jnp.concatenate([grad_values, grad_gates], axis=0).astype(jnp.bfloat16)
        input_grad = jnp.einsum('ce,enqt->cnqt', w_proj.astype(jnp.float32), grad_proj.astype(jnp.float32))
        return (running + kernel_terms, input_grad.astype(jnp.bfloat16).reshape(C, NLEN))
    start = jnp.zeros((2, C, F1, F2, F3), jnp.float32)
    summed, grads = lax.scan(one_sequence, start, (tokens, cotangent))
    return (grads, summed.reshape(2, C, NLEN).astype(jnp.bfloat16))
```

```python
import functools
import math

import jax
import jax.numpy as jnp
import numpy as np
from jax import lax
from jax.experimental import pallas as pl
from jax.experimental.pallas import tpu as pltpu
from jax.sharding import Mesh, PartitionSpec as P

BF = jnp.bfloat16
F32 = jnp.float32
F2 = 64
F3 = 128
LANES = 128


def dft_blocks(length, direction):
    ids = np.arange(length)
    angles = (ids[:, None] * ids[None, :] % length).astype(np.float32) * np.float32(
        2.0 * math.pi / length
    )
    scale = np.float32(1.0 / math.sqrt(length))
    real = np.cos(angles) * scale
    imag = direction * np.sin(angles) * scale
    return np.block([[real, -imag], [imag, real]]).astype(np.float32)


def turns(ids, modulus):
    angles = (ids % modulus).astype(np.float64) * (2.0 * math.pi / modulus)
    return np.stack([np.cos(angles), np.sin(angles)]).astype(np.float32)


def flip_matrix(size, shift):
    out = np.zeros((size, size), np.float32)
    for j in range(size):
        out[j, (size - shift - j) % size] = 1.0
    return out


def vmem_specs(count):
    return [pl.BlockSpec(memory_space=pltpu.VMEM)] * count


SMEM_SPEC = pl.BlockSpec(memory_space=pltpu.SMEM)


def call(body, out_shape, scratch, *args, smem=0, name):
    multi = isinstance(out_shape, (tuple, list))
    return pl.pallas_call(
        body,
        out_shape=out_shape,
        in_specs=[SMEM_SPEC] * smem + vmem_specs(len(args) - smem),
        out_specs=vmem_specs(len(out_shape)) if multi else vmem_specs(1)[0],
        scratch_shapes=scratch,
        compiler_params=pltpu.CompilerParams(vmem_limit_bytes=48 << 20),
        name=name,
    )(*args)


def dot(a, b):
    return jnp.dot(a, b, preferred_element_type=F32)


def loop(count, body, unroll=1):
    def step(i, carry):
        body(i)
        return carry

    lax.fori_loop(0, count, step, 0, unroll=unroll)


def loop_carry(count, body, init, unroll=1):
    return lax.fori_loop(0, count, body, init, unroll=unroll)


def lane_block(ref, i, rows=None):
    window = pl.ds(pl.multiple_of(i * LANES, LANES), LANES)
    return ref[:, window] if rows is None else ref[rows, window]


def spread_body(x_ref, out_ref, rows_ref):
    channels, blocks, _ = out_ref.shape

    def put(i):
        rows_ref[pl.ds(pl.multiple_of(i * channels, 8), channels), :] = lane_block(
            x_ref, i
        ).astype(F32)

    loop(blocks, put, 4)
    gather_rows(rows_ref, out_ref)


def gather_rows(rows_ref, out_ref):
    channels, blocks, _ = out_ref.shape

    def take(c):
        out_ref[c] = rows_ref[pl.ds(c, blocks, stride=channels), :].astype(out_ref.dtype)

    loop(channels, take, 4)


def unpack_rows(x_ref, rows_ref):
    items, blocks, _ = x_ref.shape

    def put(c):
        rows_ref[pl.ds(pl.multiple_of(c * blocks, 8), blocks), :] = x_ref[c].astype(F32)

    loop(items, put, 4)


def values_body(wv_ref, tok_ref, out_ref, rows_ref):
    channels, blocks, _ = out_ref.shape

    def put(i):
        rows_ref[pl.ds(pl.multiple_of(i * channels, 8), channels), :] = dot(
            wv_ref[...], lane_block(tok_ref, i)
        )

    loop(blocks, put, 4)
    gather_rows(rows_ref, out_ref)


def grad_body(wg_ref, wo_ref, tok_ref, cot_ref, out_ref, rows_ref):
    channels, blocks, _ = out_ref.shape

    def put(i):
        gates = dot(wg_ref[...], lane_block(tok_ref, i))
        hidden = dot(wo_ref[...], lane_block(cot_ref, i))
        rows_ref[pl.ds(pl.multiple_of(i * channels, 8), channels), :] = hidden * gates

    loop(blocks, put, 4)
    gather_rows(rows_ref, out_ref)


def rotate(re, im, cos_part, sin_part):
    return re * cos_part - im * sin_part, re * sin_part + im * cos_part


def first_stage(z_ref, m1_ref, tw_ref, rows_ref):
    count = m1_ref.shape[0]
    half = count // 2
    unpack_rows(z_ref, rows_ref)

    def step(m2, turn):
        cos_part, sin_part = turn
        x = rows_ref[pl.ds(m2, count, stride=F2), :].astype(BF)
        y = dot(m1_ref[...], x)
        re, im = rotate(y[:half], y[half:], cos_part, -sin_part)
        rows_ref[pl.ds(m2, half, stride=2 * F2), :] = re
        rows_ref[pl.ds(F2 + m2, half, stride=2 * F2), :] = im
        return rotate(cos_part, sin_part, tw_ref[2], tw_ref[3])

    loop_carry(F2, step, (tw_ref[0], tw_ref[1]), 2)


def last_stage(out_ref, m1_ref, tw_ref, rows_ref):
    count = m1_ref.shape[0]
    half = count // 2

    def step(m2, turn):
        cos_part, sin_part = turn
        re, im = rotate(
            rows_ref[pl.ds(m2, half, stride=2 * F2), :],
            rows_ref[pl.ds(F2 + m2, half, stride=2 * F2), :],
            cos_part,
            sin_part,
        )
        x = jnp.concatenate([re, im], axis=0).astype(BF)
        rows_ref[pl.ds(m2, count, stride=F2), :] = dot(m1_ref[...], x)
        return rotate(cos_part, sin_part, tw_ref[2], tw_ref[3])

    loop_carry(F2, step, (tw_ref[0], tw_ref[1]), 2)

    def put(c):
        out_ref[c] = rows_ref[pl.ds(pl.multiple_of(c * F2, 8), F2), :].astype(BF)

    loop(count, put, 4)


def to_spectrum(x, m2_ref, m3_ref, tw2_ref):
    y = dot(m2_ref[...], x)
    re, im = rotate(y[:F2], y[F2:], tw2_ref[0], -tw2_ref[1])
    return dot(jnp.concatenate([re, im], axis=1).astype(BF), m3_ref[...]).astype(BF)


def from_spectrum(re, im, m2_ref, m3_ref, tw2_ref):
    y = dot(jnp.concatenate([re, im], axis=1).astype(BF), m3_ref[...])
    re, im = rotate(y[:, :F3], y[:, F3:], tw2_ref[0], tw2_ref[1])
    return dot(m2_ref[...], jnp.concatenate([re, im], axis=0).astype(BF))


def k1_rows(k1):
    return pl.ds(pl.multiple_of(k1 * 2 * F2, 8), 2 * F2)


def forward_values_body(
    z_ref, kh_ref, m1_ref, m2_ref, m3_ref, n1_ref, n2_ref, n3_ref, tw_ref, tw2_ref,
    conv_ref, spec_ref, rows_ref,
):
    first_stage(z_ref, m1_ref, tw_ref, rows_ref)

    def step(k1):
        spec = to_spectrum(rows_ref[k1_rows(k1), :].astype(BF), m2_ref, m3_ref, tw2_ref)
        spec_ref[k1] = spec
        spec = spec.astype(F32)
        kern = kh_ref[k1]
        re, im = rotate(spec[:, :F3], spec[:, F3:], kern[:F2], kern[F2:])
        rows_ref[k1_rows(k1), :] = from_spectrum(re, im, n2_ref, n3_ref, tw2_ref)

    loop(kh_ref.shape[0], step, 4)
    last_stage(conv_ref, n1_ref, tw_ref, rows_ref)


def forward_grad_body(
    core_ref, z_ref, kh_ref, spec_ref, m1_ref, m2_ref, m3_ref, n1_ref, n2_ref, n3_ref,
    tw_ref, tw2_ref, flips_ref, lanes_ref,
    conv_ref, keep_ref, send_ref, rows_ref, terms_ref,
):
    first_stage(z_ref, m1_ref, tw_ref, rows_ref)
    count = kh_ref.shape[0]

    def step(k1):
        grad = to_spectrum(rows_ref[k1_rows(k1), :].astype(BF), m2_ref, m3_ref, tw2_ref)
        grad = grad.astype(F32)
        kern = kh_ref[k1]
        re, im = rotate(grad[:, :F3], grad[:, F3:], kern[:F2], -kern[F2:])
        rows_ref[k1_rows(k1), :] = from_spectrum(re, im, n2_ref, n3_ref, tw2_ref)
        spec = spec_ref[k1].astype(F32)
        re, im = rotate(grad[:, :F3], grad[:, F3:], spec[:, :F3], -spec[:, F3:])
        terms_ref[k1] = jnp.concatenate([re, im], axis=0).astype(BF)

    loop(count, step, 4)
    last_stage(conv_ref, n1_ref, tw_ref, rows_ref)
    on_core_zero = core_ref[0] == 0

    def mirror(k1):
        term = terms_ref[k1].astype(F32) + flipped(terms_ref, k1, flips_ref, lanes_ref)
        re, im = 0.5 * term[:F2], 0.5 * term[F2:]
        keep_ref[k1] = jnp.where(on_core_zero, re, im).astype(BF)
        send_ref[k1] = jnp.where(on_core_zero, im, re).astype(BF)

    loop(count, mirror, 4)


def flipped(ref, k1, flips_ref, lanes_ref):
    count = ref.shape[0]
    first = k1 == 0
    block = ref[jnp.where(first, 0, count - k1)]
    turned = dot(flips_ref[jnp.where(first, 1, 0)], dot(block, lanes_ref[0]).astype(BF))
    head = dot(flips_ref[jnp.where(first, 1, 0)], dot(block, lanes_ref[1]).astype(BF))
    row = lax.broadcasted_iota(jnp.int32, turned.shape, 0) % F2
    pick_head = jnp.logical_and(first, row == 0)
    return jnp.where(pick_head, head, turned)


def response_body(core_ref, own_ref, other_ref, flips_ref, lanes_ref, kh_ref, both_ref):
    on_core_zero = core_ref[0] == 0
    count = own_ref.shape[0]

    def gather(k1):
        own, other = own_ref[k1].astype(F32), other_ref[k1].astype(F32)
        both_ref[k1] = jnp.concatenate(
            [jnp.where(on_core_zero, own, other), jnp.where(on_core_zero, other, own)], axis=0
        ).astype(BF)

    loop(count, gather, 4)

    def mirror(k1):
        kh_ref[k1] = 0.5 * (
            both_ref[k1].astype(F32) + flipped(both_ref, k1, flips_ref, lanes_ref)
        )

    loop(count, mirror, 4)


def gates_body(
    wv_ref, wg_ref, wo_ref, wpg_ref, skip_ref, tok_ref, cot_ref, conv_ref,
    part_ref, own_ref, rows_ref,
):
    channels, blocks, _ = conv_ref.shape
    unpack_rows(conv_ref, rows_ref)

    def step(i):
        tok = lane_block(tok_ref, i)
        values = dot(wv_ref[...], tok).astype(BF).astype(F32)
        gates = dot(wg_ref[...], tok)
        hidden = dot(wo_ref[...], lane_block(cot_ref, i))
        conv = rows_ref[pl.ds(i, channels, stride=blocks), :]
        mixed = conv + skip_ref[...] * values
        window = pl.ds(pl.multiple_of(i * LANES, LANES), LANES)
        part_ref[:, window] = dot(wpg_ref[...], (hidden * mixed).astype(BF))
        own_ref[:, window] = (hidden * gates).astype(BF)

    loop(blocks, step, 2)


def final_body(wpv_ref, skip_ref, part_ref, own_ref, conv_ref, out_ref, rows_ref):
    channels, blocks, _ = conv_ref.shape
    unpack_rows(conv_ref, rows_ref)

    def step(i):
        window = pl.ds(pl.multiple_of(i * LANES, LANES), LANES)
        conv = rows_ref[pl.ds(i, channels, stride=blocks), :]
        grad = conv + skip_ref[...] * own_ref[:, window].astype(F32)
        out_ref[:, window] = (part_ref[:, window] + dot(wpv_ref[...], grad.astype(BF))).astype(BF)

    loop(blocks, step, 4)


def kernel_grad_body(core_ref, keep_ref, recv_ref, out_ref, rows_ref):
    channels, blocks, _ = keep_ref.shape
    core = core_ref[0]
    for ref, part in ((keep_ref, core), (recv_ref, 1 - core)):
        unpack_rows(ref, rows_ref)

        def step(i, part=part):
            window = pl.ds(pl.multiple_of(i * LANES, LANES), LANES)
            out_ref[part, :, window] = rows_ref[pl.ds(i, channels, stride=blocks), :].astype(BF)

        loop(blocks, step, 4)


SWAP = [(0, 1), (1, 0)]


def per_device(tokens, kernel, skip, w_proj, w_out, cotangent):
    first_len = lax.axis_size("seq")
    core = lax.axis_index("core")
    z_low = lax.axis_index("zl")
    channels, positions = tokens.shape[1:]
    whole = first_len * positions
    core_arr = core.astype(jnp.int32).reshape(1)
    tok = tokens.reshape(channels, positions)
    cot = cotangent.reshape(channels, positions)
    blocks = positions // LANES
    shaped = functools.partial(jax.ShapeDtypeStruct)

    bf = functools.partial(jnp.asarray, dtype=BF)
    wv = w_proj[:, :channels].T
    wg = w_proj[:, channels:].T
    wpv = w_proj[:, :channels]
    wpg = w_proj[:, channels:]
    skip_full = jnp.broadcast_to(skip[:, None], (channels, LANES))
    m1, n1 = bf(dft_blocks(first_len, -1.0)), bf(dft_blocks(first_len, 1.0))
    m2, n2 = bf(dft_blocks(F2, -1.0)), bf(dft_blocks(F2, 1.0))
    m3, n3 = bf(dft_blocks(F3, -1.0).T), bf(dft_blocks(F3, 1.0).T)
    freq = np.arange(first_len)[:, None]
    tw = jnp.asarray(
        np.concatenate(
            [
                turns(freq * np.arange(F3)[None, :], whole),
                turns(freq * F3 * np.ones((1, F3), np.int64), whole),
            ]
        )
    )
    tw2 = jnp.asarray(turns(np.arange(F2)[:, None] * np.arange(F3)[None, :], F2 * F3))
    pair = np.array([[1.0, 0.0], [0.0, -1.0]], np.float32)
    flips = bf(np.stack([np.kron(pair, flip_matrix(F2, 1)), np.kron(pair, flip_matrix(F2, 0))]))
    lanes = bf(np.stack([flip_matrix(F3, 1), flip_matrix(F3, 0)]))

    exchange = functools.partial(lax.all_to_all, split_axis=0, concat_axis=0, tiled=True)
    share = first_len
    rows = pltpu.VMEM((channels * blocks, LANES), F32)
    small_rows = pltpu.VMEM((share * blocks, LANES), F32)
    signal = shaped((channels, blocks, LANES), BF)
    comp = shaped((share, blocks, LANES), BF)

    chosen = lax.dynamic_slice(kernel, (core, z_low * share, 0), (1, share, positions))[0]
    response = call(spread_body, comp, [small_rows], chosen, name="spread")
    response = exchange(response, "seq")
    response_other = lax.ppermute(response, "core", SWAP)

    values = call(values_body, signal, [rows], wv, tok, name="values")
    values = exchange(values, ("zl", "seq"))
    grads = call(grad_body, signal, [rows], wg, w_out, tok, cot, name="grads")
    grads = exchange(grads, ("zl", "seq"))

    kh = call(
        response_body,
        shaped((first_len, 2 * F2, F3), F32),
        [pltpu.VMEM((first_len, 2 * F2, F3), BF)],
        core_arr, response, response_other, flips, lanes,
        smem=1, name="response",
    )
    z_rows = pltpu.VMEM((2 * first_len * F2, F3), F32)
    conv, spec = call(
        forward_values_body,
        (shaped((2 * first_len, F2, F3), BF), shaped((first_len, F2, 2 * F3), BF)),
        [z_rows],
        values, kh, m1, m2, m3, n1, n2, n3, tw, tw2,
        name="values_transform",
    )
    conv = exchange(conv, ("zl", "seq"))
    back, keep, send = call(
        forward_grad_body,
        (
            shaped((2 * first_len, F2, F3), BF),
            shaped((first_len, F2, F3), BF),
            shaped((first_len, F2, F3), BF),
        ),
        [z_rows, pltpu.VMEM((first_len, 2 * F2, F3), BF)],
        core_arr, grads, kh, spec, m1, m2, m3, n1, n2, n3, tw, tw2, flips, lanes,
        smem=1, name="grads_transform",
    )
    back = exchange(back, ("zl", "seq"))
    terms = keep.astype(F32) + lax.ppermute(send, "core", SWAP).astype(F32)
    terms = exchange(terms.astype(BF), "seq")
    part, own = call(
        gates_body,
        (shaped((channels, positions), F32), shaped((channels, positions), BF)),
        [rows],
        wv, wg, w_out, wpg, skip_full, tok, cot, conv,
        name="gates",
    )
    half = share // 2
    kept = lax.dynamic_slice_in_dim(terms, core * half, half, 0)
    sent = lax.dynamic_slice_in_dim(terms, (1 - core) * half, half, 0)
    kernel_grad = call(
        kernel_grad_body,
        shaped((2, half, positions), BF),
        [pltpu.VMEM((half * blocks, LANES), F32)],
        core_arr, kept, lax.ppermute(sent, "core", SWAP),
        smem=1, name="kernel_grad",
    )
    input_grad = call(
        final_body,
        shaped((channels, positions), BF),
        [rows],
        wpv, skip_full, part, own, back,
        name="final",
    )
    return input_grad.reshape(1, channels, positions), kernel_grad


def solution(mesh):
    sequences, groups = mesh.devices.shape
    fine = Mesh(mesh.devices.reshape(2, sequences // 2, groups), ("zl", "core", "seq"))
    dp = ("zl", "core")
    placed = (P(dp, None, "seq"), P(None, None, "seq"), P(), P(), P(), P(dp, None, "seq"))
    return jax.shard_map(
        per_device,
        mesh=fine,
        in_specs=placed,
        out_specs=(P(dp, None, "seq"), P(None, dp, "seq")),
        check_vma=False,
    )
```

```python
import functools
import math

import jax
import jax.numpy as jnp
import numpy as np
from jax import lax
from jax.experimental import pallas as pl
from jax.experimental.pallas import tpu as pltpu
from jax.sharding import Mesh, PartitionSpec as P

BF = jnp.bfloat16
F32 = jnp.float32
F2 = 64
F3 = 128
LANES = 128


def dft_blocks(length, direction):
    ids = np.arange(length)
    angles = (ids[:, None] * ids[None, :] % length).astype(np.float32) * np.float32(
        2.0 * math.pi / length
    )
    scale = np.float32(1.0 / math.sqrt(length))
    real = np.cos(angles) * scale
    imag = direction * np.sin(angles) * scale
    return np.block([[real, -imag], [imag, real]]).astype(np.float32)


def turns(ids, modulus):
    angles = (ids % modulus).astype(np.float64) * (2.0 * math.pi / modulus)
    return np.stack([np.cos(angles), np.sin(angles)]).astype(np.float32)


def flip_matrix(size, shift):
    out = np.zeros((size, size), np.float32)
    for j in range(size):
        out[j, (size - shift - j) % size] = 1.0
    return out


def vmem_specs(count):
    return [pl.BlockSpec(memory_space=pltpu.VMEM)] * count


SMEM_SPEC = pl.BlockSpec(memory_space=pltpu.SMEM)


def call(body, out_shape, scratch, *args, smem=0, name, micros=20):
    multi = isinstance(out_shape, (tuple, list))
    return pl.pallas_call(
        body,
        out_shape=out_shape,
        in_specs=[SMEM_SPEC] * smem + vmem_specs(len(args) - smem),
        out_specs=vmem_specs(len(out_shape)) if multi else vmem_specs(1)[0],
        scratch_shapes=scratch,
        compiler_params=pltpu.CompilerParams(vmem_limit_bytes=48 << 20),
        cost_estimate=cost(micros),
        name=name,
    )(*args)


def cost(micros):
    return pl.CostEstimate(
        flops=micros * 10**9, transcendentals=0, bytes_accessed=micros * 3 * 10**6
    )


def dot(a, b):
    return jnp.dot(a, b, preferred_element_type=F32)


def loop(count, body, unroll=1):
    def step(i, carry):
        body(i)
        return carry

    lax.fori_loop(0, count, step, 0, unroll=unroll)


def loop_carry(count, body, init, unroll=1):
    return lax.fori_loop(0, count, body, init, unroll=unroll)


def lane_block(ref, i, rows=None):
    window = pl.ds(pl.multiple_of(i * LANES, LANES), LANES)
    return ref[:, window] if rows is None else ref[rows, window]


PAD = 2
TURN = 8
BATCH = 4


def turn_row(block, signal):
    return 2 * TURN * (block // TURN) + TURN * signal + block % TURN


def lane_part(x, i):
    return x[:, i * LANES : (i + 1) * LANES]


def row_part(x, i, size):
    return x[i * size : (i + 1) * size]


def dot_first(a, b):
    return lax.dot_general(a, b, (((0,), (0,)), ((), ())), preferred_element_type=F32)


def spread_body(x_ref, out_ref, rows_ref):
    channels, blocks, _ = out_ref.shape

    def put(i):
        rows_ref[pl.ds(i * (channels + PAD), channels), :] = lane_block(x_ref, i).astype(F32)

    loop(blocks, put, 4)

    def take(c):
        out_ref[c] = rows_ref[pl.ds(c, blocks, stride=channels + PAD), :].astype(BF)

    loop(channels, take, 4)


def unpack_rows(x_ref, rows_ref, offset=0, blocks=None):
    items = x_ref.shape[0]
    blocks = blocks or x_ref.shape[1]

    def put(c):
        block = x_ref[c, offset : offset + blocks, :]
        rows_ref[pl.ds(c * (blocks + PAD), blocks), :] = block.astype(F32)

    loop(items, put, 4)


def signals_body(wp_ref, wo_ref, tok_ref, cot_ref, out_ref, values_ref, grads_ref):
    channels = out_ref.shape[0]
    pitch = channels + PAD
    for p in range(TURN // 2):
        window = slice(2 * p * LANES, (2 * p + 2) * LANES)
        both = dot_first(wp_ref[...], tok_ref[:, window])
        values = both[:channels]
        grads = dot(wo_ref[...], cot_ref[:, window]) * both[channels:]
        for side in range(2):
            at = slice((2 * p + side) * pitch, (2 * p + side) * pitch + channels)
            values_ref[at, :] = lane_part(values, side)
            grads_ref[at, :] = lane_part(grads, side)

    def take(c):
        window = pl.ds(c, TURN, stride=pitch)
        out_ref[c] = jnp.concatenate(
            [values_ref[window, :], grads_ref[window, :]], axis=0
        ).astype(BF)

    loop(channels, take, 8)


def rotate(re, im, cos_part, sin_part):
    return re * cos_part - im * sin_part, re * sin_part + im * cos_part


def first_stage(rows_ref, signal, m1_ref, tw_ref, mid_ref):
    count = m1_ref.shape[0]
    half = count // 2
    pitch, mid = 2 * F2 + PAD, F2 + PAD

    def step(j, turn):
        cos_part, sin_part = turn
        at = turn_row(2 * j, signal)
        x = jnp.concatenate(
            [rows_ref[pl.ds(at + side, count, stride=pitch), :] for side in range(2)], axis=1
        )
        y = dot(m1_ref[...], x.astype(BF))
        re, im = rotate(y[:half], y[half:], cos_part, -sin_part)
        for side in range(2):
            mid_ref[pl.ds(2 * j + side, half, stride=2 * mid), :] = lane_part(re, side)
            mid_ref[pl.ds(mid + 2 * j + side, half, stride=2 * mid), :] = lane_part(im, side)
        return rotate(cos_part, sin_part, tw_ref[2], tw_ref[3])

    loop_carry(F2 // 2, step, (tw_ref[0], tw_ref[1]), 4)


def last_stage(rows_ref, signal, m1_ref, tw_ref, mid_ref):
    count = m1_ref.shape[0]
    half = count // 2
    pitch, mid = 2 * F2 + PAD, F2 + PAD

    def step(j, turn):
        cos_part, sin_part = turn
        parts = []
        for part in range(2):
            sides = [
                mid_ref[pl.ds(part * mid + 2 * j + side, half, stride=2 * mid), :]
                for side in range(2)
            ]
            parts.append(jnp.concatenate(sides, axis=1))
        re, im = rotate(parts[0], parts[1], cos_part, sin_part)
        y = dot(m1_ref[...], jnp.concatenate([re, im], axis=0).astype(BF))
        at = turn_row(2 * j, signal)
        for side in range(2):
            rows_ref[pl.ds(at + side, count, stride=pitch), :] = lane_part(y, side)
        return rotate(cos_part, sin_part, tw_ref[2], tw_ref[3])

    loop_carry(F2 // 2, step, (tw_ref[0], tw_ref[1]), 4)


def part_rows(k1, part):
    return pl.ds((2 * k1 + part) * (F2 + PAD), F2)


def to_spectrum(mid_ref, first, m2_ref, m3_ref, tw2_ref):
    stacked = []
    for p in range(BATCH // 2):
        pair = [
            jnp.concatenate([mid_ref[part_rows(k1, 0), :], mid_ref[part_rows(k1, 1), :]], axis=0)
            for k1 in (first + 2 * p, first + 2 * p + 1)
        ]
        y = dot(m2_ref[...], jnp.concatenate(pair, axis=1).astype(BF))
        re, im = rotate(y[:F2], y[F2:], tw2_ref[0], -tw2_ref[1])
        for side in range(2):
            stacked.append(
                jnp.concatenate([lane_part(re, side), lane_part(im, side)], axis=1).astype(BF)
            )
    return dot(jnp.concatenate(stacked, axis=0), m3_ref[...]).astype(BF)


def from_spectrum(mid_ref, first, blocks, m2_ref, m3_ref, tw2_ref):
    stacked = [jnp.concatenate(block, axis=1).astype(BF) for block in blocks]
    y = dot(jnp.concatenate(stacked, axis=0), m3_ref[...])
    for p in range(BATCH // 2):
        sides = [row_part(y, 2 * p + side, F2) for side in range(2)]
        re, im = rotate(
            jnp.concatenate([lane_part(s, 0) for s in sides], axis=1),
            jnp.concatenate([lane_part(s, 1) for s in sides], axis=1),
            tw2_ref[0],
            tw2_ref[1],
        )
        z = dot(m2_ref[...], jnp.concatenate([re, im], axis=0).astype(BF))
        for side in range(2):
            k1 = first + 2 * p + side
            mid_ref[part_rows(k1, 0), :] = lane_part(z[:F2], side)
            mid_ref[part_rows(k1, 1), :] = lane_part(z[F2:], side)


def split(spec):
    spec = spec.astype(F32)
    return spec[:, :F3], spec[:, F3:]


def spectra_body(
    core_ref, z_ref, m1_ref, m2_ref, m3_ref, tw_ref, tw2_ref,
    values_ref, grads_ref, keep_ref, send_ref, rows_ref, mid_ref,
):
    count = values_ref.shape[0]
    on_core_zero = core_ref[0] == 0
    unpack_rows(z_ref, rows_ref)
    first_stage(rows_ref, 0, m1_ref, tw_ref, mid_ref)

    def values(b):
        spec = to_spectrum(mid_ref, b * BATCH, m2_ref, m3_ref, tw2_ref)
        for t in range(BATCH):
            values_ref[b * BATCH + t] = row_part(spec, t, F2)

    loop(count // BATCH, values)
    first_stage(rows_ref, 1, m1_ref, tw_ref, mid_ref)

    def grads(b):
        spec = to_spectrum(mid_ref, b * BATCH, m2_ref, m3_ref, tw2_ref)
        for t in range(BATCH):
            k1 = b * BATCH + t
            grad = row_part(spec, t, F2)
            grads_ref[k1] = grad
            value_re, value_im = split(values_ref[k1])
            re, im = rotate(*split(grad), value_re, -value_im)
            keep_ref[k1] = jnp.where(on_core_zero, re, im).astype(BF)
            send_ref[k1] = jnp.where(on_core_zero, im, re).astype(BF)

    loop(count // BATCH, grads)


def hermitian(ref, sign, flip_rows_ref, flip_lanes_ref, head_rows_ref, head_lanes_ref, store):
    count = ref.shape[0]
    head = ref[0]
    turned = dot(head_rows_ref[...], dot(head, flip_lanes_ref[...]).astype(BF))
    first = dot(head_rows_ref[...], dot(head, head_lanes_ref[...]).astype(BF))
    row = lax.broadcasted_iota(jnp.int32, turned.shape, 0)
    store(0, 0.5 * (head.astype(F32) + sign * jnp.where(row == 0, first, turned)))

    def batch(b, keep=BATCH):
        low = count - BATCH - b * BATCH
        rows = jnp.concatenate([ref[low + t] for t in range(BATCH)], axis=0)
        turned = dot(flip_rows_ref[...], dot(rows, flip_lanes_ref[...]).astype(BF))
        for t in range(keep):
            k1 = b * BATCH + 1 + t
            store(k1, 0.5 * (ref[k1].astype(F32) + sign * row_part(turned, t, F2)))

    loop(count // BATCH - 1, batch, 3)
    batch(count // BATCH - 1, BATCH - 1)


def terms_body(
    core_ref, keep_ref, recv_ref, flip_rows_ref, flip_lanes_ref, head_rows_ref, head_lanes_ref,
    out_ref, sum_ref,
):
    sign = jnp.where(core_ref[0] == 0, 1.0, -1.0)

    def add(k1):
        sum_ref[k1] = (keep_ref[k1].astype(F32) + recv_ref[k1].astype(F32)).astype(BF)

    loop(keep_ref.shape[0], add, 4)

    def store(k1, block):
        out_ref[k1] = block.astype(BF)

    hermitian(
        sum_ref, sign, flip_rows_ref, flip_lanes_ref, head_rows_ref, head_lanes_ref, store
    )


def response_body(
    core_ref, own_ref, flip_rows_ref, flip_lanes_ref, head_rows_ref, head_lanes_ref, out_ref
):
    sign = jnp.where(core_ref[0] == 0, 1.0, -1.0)

    def store(k1, block):
        out_ref[k1] = block.astype(BF)

    hermitian(
        own_ref, sign, flip_rows_ref, flip_lanes_ref, head_rows_ref, head_lanes_ref, store
    )


def inverse_body(
    core_ref, own_ref, other_ref, values_ref, grads_ref, m1_ref, m2_ref, m3_ref,
    tw_ref, tw2_ref, out_ref, rows_ref, mid_ref,
):
    on_core_zero = core_ref[0] == 0
    count = own_ref.shape[0]

    for signal, spec_ref in ((0, values_ref), (1, grads_ref)):

        def product(b, signal=signal, spec_ref=spec_ref):
            blocks = []
            for t in range(BATCH):
                k1 = b * BATCH + t
                own, other = own_ref[k1].astype(F32), other_ref[k1].astype(F32)
                kern_re = jnp.where(on_core_zero, own, other)
                kern_im = jnp.where(on_core_zero, other, own)
                if signal:
                    kern_im = -kern_im
                blocks.append(rotate(*split(spec_ref[k1]), kern_re, kern_im))
            from_spectrum(mid_ref, b * BATCH, blocks, m2_ref, m3_ref, tw2_ref)

        loop(count // BATCH, product)
        last_stage(rows_ref, signal, m1_ref, tw_ref, mid_ref)

    items, blocks, _ = out_ref.shape

    def put(c):
        out_ref[c] = rows_ref[pl.ds(c * (blocks + PAD), blocks), :].astype(BF)

    loop(items, put, 2)


def home_body(wp_ref, wo_ref, skip_ref, tok_ref, cot_ref, direct_ref, own_ref, hidden_ref):
    channels = tok_ref.shape[0]
    for p in range(TURN // 2):
        window = slice(2 * p * LANES, (2 * p + 2) * LANES)
        both = dot_first(wp_ref[...], tok_ref[:, window])
        values, gates = both[:channels].astype(BF).astype(F32), both[channels:]
        hidden = dot(wo_ref[...], cot_ref[:, window])
        direct_ref[:, window] = skip_ref[...] * values
        own_ref[:, window] = skip_ref[...] * (hidden * gates).astype(BF).astype(F32)
        hidden_ref[:, window] = hidden


def final_body(wp_ref, direct_ref, own_ref, hidden_ref, got_ref, out_ref, rows_ref):
    channels = got_ref.shape[0]
    pitch = 2 * TURN + PAD
    unpack_rows(got_ref, rows_ref)
    for p in range(TURN // 2):
        window = slice(2 * p * LANES, (2 * p + 2) * LANES)
        conv, back = (
            jnp.concatenate(
                [
                    rows_ref[pl.ds(signal * TURN + 2 * p + side, channels, stride=pitch), :]
                    for side in range(2)
                ],
                axis=1,
            )
            for signal in range(2)
        )
        grad = back + own_ref[:, window]
        mixed = conv + direct_ref[:, window]
        stacked = jnp.concatenate([grad, hidden_ref[:, window] * mixed], axis=0).astype(BF)
        out_ref[:, window] = dot(wp_ref[...], stacked).astype(BF)


def chunked(body, name, micros, small, chunks, outs, messages=(), scratch=()):
    steps = chunks[0].shape[1] // (TURN * LANES)
    whole = [pl.BlockSpec(a.shape, lambda i: (0, 0)) for a in small]
    wide = lambda a: pl.BlockSpec((a.shape[0], TURN * LANES), lambda i: (0, i))
    turn = lambda a: pl.BlockSpec((a.shape[0], 2 * TURN, LANES), lambda i: (0, i, 0))
    spec = lambda a: wide(a) if len(a.shape) == 2 else turn(a)
    result = pl.pallas_call(
        body,
        grid=(steps,),
        out_shape=outs,
        in_specs=whole + [spec(a) for a in chunks + tuple(messages)],
        out_specs=[spec(a) for a in outs],
        scratch_shapes=list(scratch),
        compiler_params=pltpu.CompilerParams(vmem_limit_bytes=32 << 20),
        cost_estimate=cost(micros),
        name=name,
    )(*small, *(in_hbm(a) for a in chunks + tuple(messages)))
    return result


def in_hbm(a):
    return pltpu.with_memory_space_constraint(a, pltpu.HBM)


def kernel_grad_body(core_ref, keep_ref, recv_ref, out_ref, rows_ref):
    channels, blocks, _ = keep_ref.shape
    core = core_ref[0]
    for ref, part in ((keep_ref, core), (recv_ref, 1 - core)):
        unpack_rows(ref, rows_ref)

        def step(i, part=part):
            window = pl.ds(pl.multiple_of(i * LANES, LANES), LANES)
            rows = rows_ref[pl.ds(i, channels, stride=blocks + PAD), :]
            out_ref[part, :, window] = rows.astype(BF)

        loop(blocks, step, 4)


SWAP = [(0, 1), (1, 0)]


def per_device(tokens, kernel, skip, w_proj, w_out, cotangent):
    first_len = lax.axis_size("seq")
    core = lax.axis_index("core")
    z_low = lax.axis_index("zl")
    channels, positions = tokens.shape[1:]
    whole = first_len * positions
    core_arr = core.astype(jnp.int32).reshape(1)
    tok = tokens.reshape(channels, positions)
    cot = cotangent.reshape(channels, positions)
    blocks = positions // LANES
    shaped = functools.partial(jax.ShapeDtypeStruct)

    bf = functools.partial(jnp.asarray, dtype=BF)
    skip_full = jnp.broadcast_to(skip[:, None], (channels, 2 * LANES))
    m1, n1 = bf(dft_blocks(first_len, -1.0)), bf(dft_blocks(first_len, 1.0))
    m2, n2 = bf(dft_blocks(F2, -1.0)), bf(dft_blocks(F2, 1.0))
    m3, n3 = bf(dft_blocks(F3, -1.0).T), bf(dft_blocks(F3, 1.0).T)
    freq = np.arange(first_len)[:, None]
    pair = np.arange(2 * F3)[None, :]
    tw = jnp.asarray(
        np.concatenate(
            [turns(freq * pair, whole), turns(freq * np.full_like(pair, 2 * F3), whole)]
        )
    )
    tw2 = turns(np.arange(F2)[:, None] * np.arange(F3)[None, :], F2 * F3)
    tw2 = jnp.asarray(np.concatenate([tw2, tw2], axis=2))
    flips = (
        bf(flip_matrix(BATCH * F2, 1)),
        bf(flip_matrix(F3, 1)),
        bf(flip_matrix(F2, 0)),
        bf(flip_matrix(F3, 0)),
    )

    exchange = functools.partial(lax.all_to_all, split_axis=0, concat_axis=0, tiled=True)
    share = first_len
    half = share // 2
    pair_rows = pltpu.VMEM((2 * first_len * (2 * F2 + PAD), F3), F32)
    mid_rows = pltpu.VMEM((2 * first_len * (F2 + PAD), F3), F32)
    part = shaped((share, blocks, LANES), BF)

    turn_rows = pltpu.VMEM((TURN * (channels + PAD), LANES), F32)
    (signals,) = chunked(
        signals_body, "signals", 8, (w_proj, w_out), (tok, cot),
        (pltpu.HBM((channels, 2 * blocks, LANES), BF),), (), (turn_rows, turn_rows),
    )
    signals = exchange(signals, ("zl", "seq"))
    chosen = lax.dynamic_slice(kernel, (core, z_low * share, 0), (1, share, positions))[0]
    response = call(
        spread_body, part, [pltpu.VMEM((blocks * (share + PAD), LANES), F32)],
        chosen, name="spread", micros=3,
    )
    response, signals = lax.optimization_barrier((response, signals))
    response = exchange(response, "seq")
    spectrum = shaped((first_len, F2, 2 * F3), BF)
    values, grads, keep, send = call(
        spectra_body,
        (spectrum, spectrum, part, part),
        [pair_rows, mid_rows],
        core_arr, signals, m1, m2, m3, tw, tw2,
        smem=1, name="spectra", micros=20,
    )
    terms = call(
        terms_body, part, [pltpu.VMEM((first_len, F2, F3), BF)],
        core_arr, keep, lax.ppermute(send, "core", SWAP), *flips,
        smem=1, name="terms", micros=4,
    )
    terms, response = lax.optimization_barrier((terms, response))
    terms = exchange(terms, "seq")
    response = call(
        response_body, part, [], core_arr, response, *flips, smem=1, name="response", micros=4
    )
    received = call(
        inverse_body,
        shaped((2 * first_len, 2 * F2, F3), BF),
        [pair_rows, mid_rows],
        core_arr, response, lax.ppermute(response, "core", SWAP), values, grads,
        n1, n2, n3, tw, tw2,
        smem=1, name="inverse", micros=20,
    )
    received, terms = lax.optimization_barrier((received, terms))
    received = exchange(received, ("zl", "seq"))
    kept = lax.dynamic_slice_in_dim(terms, core * half, half, 0)
    sent = lax.dynamic_slice_in_dim(terms, (1 - core) * half, half, 0)
    kernel_grad = call(
        kernel_grad_body,
        shaped((2, half, positions), BF),
        [pltpu.VMEM((half * (blocks + PAD), LANES), F32)],
        core_arr, kept, lax.ppermute(sent, "core", SWAP),
        smem=1, name="kernel_grad", micros=3,
    )
    wide = pltpu.HBM((channels, positions), F32)
    direct, own, hidden = chunked(
        home_body, "home", 8, (w_proj, w_out, skip_full), (tok, cot), (wide, wide, wide)
    )
    (input_grad,) = chunked(
        final_body, "final", 8, (w_proj,), (direct, own, hidden),
        (pltpu.HBM((channels, positions), BF),), (received,),
        (pltpu.VMEM((channels * (2 * TURN + PAD), LANES), F32),),
    )
    return input_grad.reshape(1, channels, positions), kernel_grad


def solution(mesh):
    sequences, groups = mesh.devices.shape
    fine = Mesh(mesh.devices.reshape(2, sequences // 2, groups), ("zl", "core", "seq"))
    dp = ("zl", "core")
    placed = (P(dp, None, "seq"), P(None, None, "seq"), P(), P(), P(), P(dp, None, "seq"))
    return jax.shard_map(
        per_device,
        mesh=fine,
        in_specs=placed,
        out_specs=(P(dp, None, "seq"), P(None, dp, "seq")),
        check_vma=False,
    )
```

```python
import functools
import math

import jax
import jax.numpy as jnp
import numpy as np
from jax import lax
from jax.experimental import pallas as pl
from jax.experimental.pallas import tpu as pltpu
from jax.sharding import Mesh, PartitionSpec as P


BF = jnp.bfloat16
F32 = jnp.float32
F2 = 64
F3 = 128
LANES = 128


def dft_blocks(length, direction):
    ids = np.arange(length)
    angles = (ids[:, None] * ids[None, :] % length).astype(np.float32) * np.float32(
        2.0 * math.pi / length
    )
    scale = np.float32(1.0 / math.sqrt(length))
    real = np.cos(angles) * scale
    imag = direction * np.sin(angles) * scale
    return np.block([[real, -imag], [imag, real]]).astype(np.float32)


def turns(ids, modulus):
    angles = (ids % modulus).astype(np.float64) * (2.0 * math.pi / modulus)
    return np.stack([np.cos(angles), np.sin(angles)]).astype(np.float32)


def flip_matrix(size, shift):
    row = lax.broadcasted_iota(jnp.int32, (size, size), 0)
    column = lax.broadcasted_iota(jnp.int32, (size, size), 1)
    total = row + column
    hit = total == size - shift
    if not shift:
        hit = jnp.logical_or(hit, total == 0)
    return jnp.where(hit, 1.0, 0.0).astype(BF)


def vmem_specs(count):
    return [pl.BlockSpec(memory_space=pltpu.VMEM)] * count


SMEM_SPEC = pl.BlockSpec(memory_space=pltpu.SMEM)


def call(body, out_shape, scratch, *args, smem=0, micros=20):
    multi = isinstance(out_shape, (tuple, list))
    return pl.pallas_call(
        body,
        out_shape=out_shape,
        in_specs=[SMEM_SPEC] * smem + vmem_specs(len(args) - smem),
        out_specs=vmem_specs(len(out_shape)) if multi else vmem_specs(1)[0],
        scratch_shapes=scratch,
        compiler_params=pltpu.CompilerParams(vmem_limit_bytes=48 << 20),
        cost_estimate=cost(micros),
    )(*args)


def cost(micros):
    return pl.CostEstimate(
        flops=micros * 10**9, transcendentals=0, bytes_accessed=micros * 3 * 10**6
    )


def dot(a, b):
    return jnp.dot(a, b, preferred_element_type=F32)


def loop(count, body, unroll=1):
    def step(i, carry):
        body(i)
        return carry

    lax.fori_loop(0, count, step, 0, unroll=unroll)


def loop_carry(count, body, init, unroll=1):
    return lax.fori_loop(0, count, body, init, unroll=unroll)


def lane_block(ref, i, rows=None):
    window = pl.ds(pl.multiple_of(i * LANES, LANES), LANES)
    return ref[:, window] if rows is None else ref[rows, window]


PAD = 2
TURN = 8
BATCH = 4


def lane_part(x, i):
    return x[:, i * LANES : (i + 1) * LANES]


def row_part(x, i, size):
    return x[i * size : (i + 1) * size]


def spread_body(x_ref, out_ref, rows_ref):
    channels, blocks, _ = out_ref.shape

    def put(i):
        rows_ref[pl.ds(i * (channels + PAD), channels), :] = lane_block(x_ref, i).astype(F32)

    loop(blocks, put, 4)

    def take(c):
        out_ref[c] = rows_ref[pl.ds(c, blocks, stride=channels + PAD), :].astype(BF)

    loop(channels, take, 4)


def unpack_rows(x_ref, rows_ref, offset=0, blocks=None):
    items = x_ref.shape[0]
    blocks = blocks or x_ref.shape[1]

    def put(c):
        block = x_ref[c, offset : offset + blocks, :]
        rows_ref[pl.ds(c * (blocks + PAD), blocks), :] = block.astype(F32)

    loop(items, put, 4)


def take_turn(rows_ref, out_ref):
    channels = out_ref.shape[0]

    def take(c):
        out_ref[c] = rows_ref[pl.ds(c, TURN, stride=channels + PAD), :].astype(BF)

    loop(channels, take, 8)


def put_pair(rows_ref, pair, x):
    channels = x.shape[0]
    pitch = channels + PAD
    for side in range(2):
        at = (2 * pair + side) * pitch
        rows_ref[at : at + channels, :] = lane_part(x, side)


def pair_window(pair):
    return slice(2 * pair * LANES, (2 * pair + 2) * LANES)


def values_body(wv_ref, tok_ref, out_ref, rows_ref):
    for p in range(TURN // 2):
        put_pair(rows_ref, p, dot(wv_ref[...], tok_ref[:, pair_window(p)]))
    take_turn(rows_ref, out_ref)


def grads_body(wg_ref, wo_ref, tok_ref, cot_ref, out_ref, rows_ref):
    for p in range(TURN // 2):
        gates = dot(wg_ref[...], tok_ref[:, pair_window(p)])
        put_pair(rows_ref, p, dot(wo_ref[...], cot_ref[:, pair_window(p)]) * gates)
    take_turn(rows_ref, out_ref)


def rotate(re, im, cos_part, sin_part):
    return re * cos_part - im * sin_part, re * sin_part + im * cos_part


def first_stage(rows_ref, m1_ref, tw_ref, mid_ref):
    count = m1_ref.shape[0]
    half = count // 2
    mid = F2 + PAD

    def step(j, turn):
        cos_part, sin_part = turn
        x = jnp.concatenate(
            [rows_ref[pl.ds(2 * j + side, count, stride=mid), :] for side in range(2)], axis=1
        )
        y = dot(m1_ref[...], x.astype(BF))
        re, im = rotate(y[:half], y[half:], cos_part, -sin_part)
        for side in range(2):
            mid_ref[pl.ds(2 * j + side, half, stride=2 * mid), :] = lane_part(re, side)
            mid_ref[pl.ds(mid + 2 * j + side, half, stride=2 * mid), :] = lane_part(im, side)
        return rotate(cos_part, sin_part, tw_ref[2], tw_ref[3])

    loop_carry(F2 // 2, step, (tw_ref[0], tw_ref[1]), 2)


def last_stage(rows_ref, m1_ref, tw_ref, mid_ref):
    count = m1_ref.shape[0]
    half = count // 2
    mid = F2 + PAD

    def step(j, turn):
        cos_part, sin_part = turn
        parts = []
        for part in range(2):
            sides = [
                mid_ref[pl.ds(part * mid + 2 * j + side, half, stride=2 * mid), :]
                for side in range(2)
            ]
            parts.append(jnp.concatenate(sides, axis=1))
        re, im = rotate(parts[0], parts[1], cos_part, sin_part)
        y = dot(m1_ref[...], jnp.concatenate([re, im], axis=0).astype(BF))
        for side in range(2):
            rows_ref[pl.ds(2 * j + side, count, stride=mid), :] = lane_part(y, side)
        return rotate(cos_part, sin_part, tw_ref[2], tw_ref[3])

    loop_carry(F2 // 2, step, (tw_ref[0], tw_ref[1]), 2)


def part_rows(k1, part):
    return pl.ds((2 * k1 + part) * (F2 + PAD), F2)


def to_spectrum(mid_ref, first, m2_ref, m3_ref, tw2_ref):
    stacked = []
    for p in range(BATCH // 2):
        pair = [
            jnp.concatenate([mid_ref[part_rows(k1, 0), :], mid_ref[part_rows(k1, 1), :]], axis=0)
            for k1 in (first + 2 * p, first + 2 * p + 1)
        ]
        y = dot(m2_ref[...], jnp.concatenate(pair, axis=1).astype(BF))
        re, im = rotate(y[:F2], y[F2:], tw2_ref[0], -tw2_ref[1])
        for side in range(2):
            stacked.append(
                jnp.concatenate([lane_part(re, side), lane_part(im, side)], axis=1).astype(BF)
            )
    return dot(jnp.concatenate(stacked, axis=0), m3_ref[...]).astype(BF)


def from_spectrum(mid_ref, first, blocks, m2_ref, m3_ref, tw2_ref):
    stacked = [jnp.concatenate(block, axis=1).astype(BF) for block in blocks]
    y = dot(jnp.concatenate(stacked, axis=0), m3_ref[...])
    for p in range(BATCH // 2):
        sides = [row_part(y, 2 * p + side, F2) for side in range(2)]
        re, im = rotate(
            jnp.concatenate([lane_part(s, 0) for s in sides], axis=1),
            jnp.concatenate([lane_part(s, 1) for s in sides], axis=1),
            tw2_ref[0],
            tw2_ref[1],
        )
        z = dot(m2_ref[...], jnp.concatenate([re, im], axis=0).astype(BF))
        for side in range(2):
            k1 = first + 2 * p + side
            mid_ref[part_rows(k1, 0), :] = lane_part(z[:F2], side)
            mid_ref[part_rows(k1, 1), :] = lane_part(z[F2:], side)


def split(spec):
    spec = spec.astype(F32)
    return spec[:, :F3], spec[:, F3:]


def kernel_parts(core_ref, own_ref, other_ref, k1):
    own, other = own_ref[k1].astype(F32), other_ref[k1].astype(F32)
    on_core_zero = core_ref[0] == 0
    return jnp.where(on_core_zero, own, other), jnp.where(on_core_zero, other, own)


def pack_rows(rows_ref, out_ref):
    items, blocks, _ = out_ref.shape

    def put(c):
        out_ref[c] = rows_ref[pl.ds(c * (blocks + PAD), blocks), :].astype(BF)

    loop(items, put, 4)


def values_transform_body(
    core_ref, z_ref, own_ref, other_ref, m1_ref, m2_ref, m3_ref, n1_ref, n2_ref, n3_ref,
    tw_ref, tw2_ref, out_ref, spec_ref, rows_ref, mid_ref,
):
    count = spec_ref.shape[0]
    unpack_rows(z_ref, rows_ref)
    first_stage(rows_ref, m1_ref, tw_ref, mid_ref)

    def spectrum(b):
        spec = to_spectrum(mid_ref, b * BATCH, m2_ref, m3_ref, tw2_ref)
        for t in range(BATCH):
            spec_ref[b * BATCH + t] = row_part(spec, t, F2)

    loop(count // BATCH, spectrum)

    def product(b):
        blocks = []
        for t in range(BATCH):
            k1 = b * BATCH + t
            kern_re, kern_im = kernel_parts(core_ref, own_ref, other_ref, k1)
            blocks.append(rotate(*split(spec_ref[k1]), kern_re, kern_im))
        from_spectrum(mid_ref, b * BATCH, blocks, n2_ref, n3_ref, tw2_ref)

    loop(count // BATCH, product)
    last_stage(rows_ref, n1_ref, tw_ref, mid_ref)
    pack_rows(rows_ref, out_ref)


def grads_transform_body(
    core_ref, z_ref, own_ref, other_ref, values_ref, m1_ref, m2_ref, m3_ref, n1_ref, n2_ref,
    n3_ref, tw_ref, tw2_ref, out_ref, keep_ref, send_ref, rows_ref, mid_ref, spec_ref,
):
    count = values_ref.shape[0]
    on_core_zero = core_ref[0] == 0
    unpack_rows(z_ref, rows_ref)
    first_stage(rows_ref, m1_ref, tw_ref, mid_ref)

    def spectrum(b):
        spec = to_spectrum(mid_ref, b * BATCH, m2_ref, m3_ref, tw2_ref)
        for t in range(BATCH):
            k1 = b * BATCH + t
            grad = row_part(spec, t, F2)
            spec_ref[k1] = grad
            value_re, value_im = split(values_ref[k1])
            re, im = rotate(*split(grad), value_re, -value_im)
            keep_ref[k1] = jnp.where(on_core_zero, re, im).astype(BF)
            send_ref[k1] = jnp.where(on_core_zero, im, re).astype(BF)

    loop(count // BATCH, spectrum)

    def product(b):
        blocks = []
        for t in range(BATCH):
            k1 = b * BATCH + t
            kern_re, kern_im = kernel_parts(core_ref, own_ref, other_ref, k1)
            blocks.append(rotate(*split(spec_ref[k1]), kern_re, -kern_im))
        from_spectrum(mid_ref, b * BATCH, blocks, n2_ref, n3_ref, tw2_ref)

    loop(count // BATCH, product)
    last_stage(rows_ref, n1_ref, tw_ref, mid_ref)
    pack_rows(rows_ref, out_ref)


def hermitian(ref, sign, flip_rows_ref, flip_lanes_ref, store):
    count = ref.shape[0]
    flip_rows_ref[...] = flip_matrix(BATCH * F2, 1)
    flip_lanes_ref[...] = flip_matrix(F3, 1)
    head = ref[0]
    head_rows = flip_matrix(F2, 0)
    turned = dot(head_rows, dot(head, flip_lanes_ref[...]).astype(BF))
    first = dot(head_rows, dot(head, flip_matrix(F3, 0)).astype(BF))
    row = lax.broadcasted_iota(jnp.int32, turned.shape, 0)
    store(0, 0.5 * (head.astype(F32) + sign * jnp.where(row == 0, first, turned)))

    def batch(b, keep=BATCH):
        low = count - BATCH - b * BATCH
        rows = jnp.concatenate([ref[low + t] for t in range(BATCH)], axis=0)
        turned = dot(flip_rows_ref[...], dot(rows, flip_lanes_ref[...]).astype(BF))
        for t in range(keep):
            k1 = b * BATCH + 1 + t
            store(k1, 0.5 * (ref[k1].astype(F32) + sign * row_part(turned, t, F2)))

    loop(count // BATCH - 1, batch, 3)
    batch(count // BATCH - 1, BATCH - 1)


def terms_body(
    core_ref, keep_ref, recv_ref, out_ref, sum_ref, flip_rows_ref, flip_lanes_ref
):
    sign = jnp.where(core_ref[0] == 0, 1.0, -1.0)

    def add(k1):
        sum_ref[k1] = (keep_ref[k1].astype(F32) + recv_ref[k1].astype(F32)).astype(BF)

    loop(keep_ref.shape[0], add, 4)

    def store(k1, block):
        out_ref[k1] = block.astype(BF)

    hermitian(sum_ref, sign, flip_rows_ref, flip_lanes_ref, store)


def slot(place_ref, index, size, axes=3):
    at = 0
    for axis in range(3 - axes, 3):
        digit = lax.rem(lax.div(index, size ** (2 - axis)), size)
        at = at * size + lax.rem(place_ref[1 + axis] - digit + size, size)
    return at


def response_body(
    size, place_ref, got_ref, out_ref, own_ref, flip_rows_ref, flip_lanes_ref
):
    sign = jnp.where(place_ref[0] == 0, 1.0, -1.0)

    def order(k1):
        own_ref[k1] = got_ref[slot(place_ref, k1, size)]

    loop(own_ref.shape[0], order, 4)

    def store(k1, block):
        out_ref[k1] = block.astype(BF)

    hermitian(own_ref, sign, flip_rows_ref, flip_lanes_ref, store)


def gather_pair(rows_ref, pair, channels):
    return jnp.concatenate(
        [rows_ref[pl.ds(2 * pair + side, channels, stride=TURN + PAD), :] for side in range(2)],
        axis=1,
    )


def gates_body(
    wv_ref, wg_ref, wo_ref, wpg_ref, skip_ref, tok_ref, cot_ref, conv_ref,
    part_ref, own_ref, rows_ref,
):
    channels = conv_ref.shape[0]
    unpack_rows(conv_ref, rows_ref)
    for p in range(TURN // 2):
        window = pair_window(p)
        tok = tok_ref[:, window]
        values = dot(wv_ref[...], tok).astype(BF).astype(F32)
        hidden = dot(wo_ref[...], cot_ref[:, window])
        own = (hidden * dot(wg_ref[...], tok)).astype(BF).astype(F32)
        mixed = gather_pair(rows_ref, p, channels) + skip_ref[...] * values
        part_ref[:, window] = dot(wpg_ref[...], (hidden * mixed).astype(BF))
        own_ref[:, window] = skip_ref[...] * own


def final_body(wpv_ref, part_ref, own_ref, back_ref, out_ref, rows_ref):
    channels = back_ref.shape[0]
    unpack_rows(back_ref, rows_ref)
    for p in range(TURN // 2):
        window = pair_window(p)
        grad = gather_pair(rows_ref, p, channels) + own_ref[:, window]
        out_ref[:, window] = (part_ref[:, window] + dot(wpv_ref[...], grad.astype(BF))).astype(BF)


def chunked(body, micros, small, chunks, outs, messages=(), scratch=()):
    steps = chunks[0].shape[1] // (TURN * LANES)
    whole = [pl.BlockSpec(a.shape, lambda i: (0, 0)) for a in small]
    wide = lambda a: pl.BlockSpec((a.shape[0], TURN * LANES), lambda i: (0, i))
    turn = lambda a: pl.BlockSpec((a.shape[0], TURN, LANES), lambda i: (0, i, 0))
    spec = lambda a: wide(a) if len(a.shape) == 2 else turn(a)
    return pl.pallas_call(
        body,
        grid=(steps,),
        out_shape=outs,
        in_specs=whole + [spec(a) for a in chunks + tuple(messages)],
        out_specs=[spec(a) for a in outs],
        scratch_shapes=list(scratch),
        compiler_params=pltpu.CompilerParams(vmem_limit_bytes=32 << 20),
        cost_estimate=cost(micros),
    )(*small, *(in_hbm(a) for a in chunks + tuple(messages)))


def in_hbm(a):
    return pltpu.with_memory_space_constraint(a, pltpu.HBM)


def kernel_grad_body(size, place_ref, keep_ref, recv_ref, out_ref, rows_ref):
    channels, blocks, _ = keep_ref.shape
    core = place_ref[0]
    for ref, part in ((keep_ref, core), (recv_ref, 1 - core)):

        def put(c, ref=ref):
            at = lax.div(c, size * size) * size * size + slot(place_ref, c, size, 2)
            rows_ref[pl.ds(c * (blocks + PAD), blocks), :] = ref[at].astype(F32)

        loop(channels, put, 4)

        def step(i, part=part):
            window = pl.ds(pl.multiple_of(i * LANES, LANES), LANES)
            rows = rows_ref[pl.ds(i, channels, stride=blocks + PAD), :]
            out_ref[part, :, window] = rows.astype(BF)

        loop(blocks, step, 4)


SWAP = [(0, 1), (1, 0)]
RING = ("zh", "y", "x")
SEQ = RING
GROUP = ("zl",) + RING


def ring_step(y, axis, size):
    me = lax.axis_index(RING[axis])
    parts = []
    for step in range(size):
        slab = lax.dynamic_slice_in_dim(y, lax.rem(me + step, size), 1, axis)
        ring = [(i, (i + step) % size) for i in range(size)]
        parts.append(lax.ppermute(slab, RING[axis], ring) if step else slab)
    return jnp.concatenate(parts, axis=axis)


def cube(x, size):
    return x.reshape((size, size, size) + x.shape[1:])


def exchange(x):
    return lax.all_to_all(x, GROUP, split_axis=0, concat_axis=0, tiled=True)


def per_device(tokens, kernel, skip, w_proj, w_out, cotangent):
    size = lax.axis_size("x")
    first_len = size**3
    core = lax.axis_index("core")
    z_low = lax.axis_index("zl")
    channels, positions = tokens.shape[1:]
    whole = first_len * positions
    place = jnp.stack([core] + [lax.axis_index(name) for name in RING]).astype(jnp.int32)
    tok = tokens.reshape(channels, positions)
    cot = cotangent.reshape(channels, positions)
    blocks = positions // LANES
    shaped = jax.ShapeDtypeStruct

    bf = functools.partial(jnp.asarray, dtype=BF)
    skip_full = jnp.broadcast_to(skip[:, None], (channels, 2 * LANES))
    m1, n1 = bf(dft_blocks(first_len, -1.0)), bf(dft_blocks(first_len, 1.0))
    m2, n2 = bf(dft_blocks(F2, -1.0)), bf(dft_blocks(F2, 1.0))
    m3, n3 = bf(dft_blocks(F3, -1.0).T), bf(dft_blocks(F3, 1.0).T)
    freq = np.arange(first_len)[:, None]
    pair = np.arange(2 * F3)[None, :]
    tw = jnp.asarray(
        np.concatenate(
            [turns(freq * pair, whole), turns(freq * np.full_like(pair, 2 * F3), whole)]
        )
    )
    tw2 = turns(np.arange(F2)[:, None] * np.arange(F3)[None, :], F2 * F3)
    tw2 = jnp.asarray(np.concatenate([tw2, tw2], axis=2))
    share = first_len
    half = share // 2
    mid_rows = pltpu.VMEM((2 * first_len * (F2 + PAD), F3), F32)
    turn_rows = pltpu.VMEM((TURN * (channels + PAD), LANES), F32)
    turn_items = pltpu.VMEM((channels * (TURN + PAD), LANES), F32)
    part = shaped((share, blocks, LANES), BF)
    flip_scratch = [
        pltpu.VMEM((first_len, F2, F3), BF),
        pltpu.VMEM((BATCH * F2, BATCH * F2), BF),
        pltpu.VMEM((F3, F3), BF),
    ]
    message = pltpu.HBM((channels, blocks, LANES), BF)
    spectrum = shaped((first_len, F2, 2 * F3), BF)
    wv, wg = w_proj[:, :channels].T, w_proj[:, channels:].T
    wpv, wpg = w_proj[:, :channels], w_proj[:, channels:]

    (values,) = chunked(values_body, 5, (wv,), (tok,), (message,), (), (turn_rows,))
    values = exchange(values)

    chosen = lax.dynamic_slice(kernel, (core, z_low * share, 0), (1, share, positions))[0]
    response = call(
        spread_body, part, [pltpu.VMEM((blocks * (share + PAD), LANES), F32)],
        chosen, micros=3,
    )
    response = ring_step(cube(response, size), 2, size)
    (grads,) = chunked(grads_body, 6, (wg, w_out), (tok, cot), (message,), (), (turn_rows,))
    grads, response = lax.optimization_barrier((grads, response))
    response = ring_step(ring_step(response, 1, size), 0, size)
    grads, values = lax.optimization_barrier((grads, values))
    grads = exchange(grads)
    response = call(
        functools.partial(response_body, size), part, flip_scratch,
        place, response.reshape(part.shape),
        smem=1, micros=4,
    )
    other = lax.ppermute(response, "core", SWAP)
    tables = (m1, m2, m3, n1, n2, n3, tw, tw2)
    conv, spec = call(
        values_transform_body, (message, spectrum), [mid_rows, mid_rows],
        place, values, response, other, *tables,
        smem=1, micros=20,
    )
    conv, grads = lax.optimization_barrier((conv, grads))
    conv = exchange(conv)
    back, keep, send = call(
        grads_transform_body, (message, part, part),
        [mid_rows, mid_rows, pltpu.VMEM((first_len, F2, 2 * F3), BF)],
        place, grads, response, other, spec, *tables,
        smem=1, micros=22,
    )
    terms = call(
        terms_body, part, flip_scratch,
        place, keep, lax.ppermute(send, "core", SWAP),
        smem=1, micros=5,
    )
    terms = ring_step(cube(terms, size), 0, size)
    back, conv = lax.optimization_barrier((back, conv))
    back = exchange(back)
    gates, own = chunked(
        gates_body, 10, (wv, wg, w_out, wpg, skip_full), (tok, cot),
        (pltpu.HBM((channels, positions), F32),) * 2, (conv,), (turn_items,),
    )
    terms = ring_step(ring_step(terms, 1, size), 2, size)
    me = lax.axis_index(RING[0])

    def halves(of_core):
        slabs = [
            lax.dynamic_slice_in_dim(terms, lax.rem(me - of_core * (size // 2) - i + size, size), 1, 0)
            for i in range(size // 2)
        ]
        return jnp.concatenate(slabs, axis=0).reshape(half, blocks, LANES)

    kernel_grad = call(
        functools.partial(kernel_grad_body, size),
        shaped((2, half, positions), BF),
        [pltpu.VMEM((half * (blocks + PAD), LANES), F32)],
        place, halves(core), lax.ppermute(halves(1 - core), "core", SWAP),
        smem=1, micros=3,
    )
    (input_grad,) = chunked(
        final_body, 6, (wpv,), (gates, own),
        (pltpu.HBM((channels, positions), BF),), (back,), (turn_items,),
    )
    return input_grad.reshape(1, channels, positions), kernel_grad


def solution(mesh):
    sequences, groups = mesh.devices.shape
    size = round(groups ** (1 / 3))
    fine = Mesh(
        mesh.devices.reshape(2, sequences // 2, size, size, size), ("zl", "core") + RING
    )
    dp = ("zl", "core")
    signal = P(dp, None, SEQ)
    return jax.shard_map(
        per_device,
        mesh=fine,
        in_specs=(signal, P(None, None, SEQ), P(), P(), P(), signal),
        out_specs=(signal, P(None, dp, SEQ)),
        check_vma=False,
    )
```

```python
import functools
import math

import jax
import jax.numpy as jnp
import numpy as np
from jax import lax
from jax.experimental import pallas as pl
from jax.experimental.pallas import tpu as pltpu
from jax.sharding import Mesh, PartitionSpec as P


BF = jnp.bfloat16
F32 = jnp.float32
F2 = 64
F3 = 128
LANES = 128


def dft_blocks(length, direction):
    ids = np.arange(length)
    angles = (ids[:, None] * ids[None, :] % length).astype(np.float32) * np.float32(
        2.0 * math.pi / length
    )
    scale = np.float32(1.0 / math.sqrt(length))
    real = np.cos(angles) * scale
    imag = direction * np.sin(angles) * scale
    return np.block([[real, -imag], [imag, real]]).astype(np.float32)


def turns(ids, modulus):
    angles = (ids % modulus).astype(np.float64) * (2.0 * math.pi / modulus)
    return np.stack([np.cos(angles), np.sin(angles)]).astype(np.float32)


def flip_matrix(size, shift):
    row = lax.broadcasted_iota(jnp.int32, (size, size), 0)
    column = lax.broadcasted_iota(jnp.int32, (size, size), 1)
    total = row + column
    hit = total == size - shift
    if not shift:
        hit = jnp.logical_or(hit, total == 0)
    return jnp.where(hit, 1.0, 0.0).astype(BF)


def vmem_specs(count):
    return [pl.BlockSpec(memory_space=pltpu.VMEM)] * count


SMEM_SPEC = pl.BlockSpec(memory_space=pltpu.SMEM)


def call(body, out_shape, scratch, *args, smem=0, micros=20):
    multi = isinstance(out_shape, (tuple, list))
    return pl.pallas_call(
        body,
        out_shape=out_shape,
        in_specs=[SMEM_SPEC] * smem + vmem_specs(len(args) - smem),
        out_specs=vmem_specs(len(out_shape)) if multi else vmem_specs(1)[0],
        scratch_shapes=scratch,
        compiler_params=pltpu.CompilerParams(vmem_limit_bytes=48 << 20),
        cost_estimate=cost(micros),
    )(*args)


def cost(micros):
    return pl.CostEstimate(
        flops=micros * 10**9, transcendentals=0, bytes_accessed=micros * 3 * 10**6
    )


def dot(a, b):
    return jnp.dot(a, b, preferred_element_type=F32)


def loop(count, body, unroll=1):
    def step(i, carry):
        body(i)
        return carry

    lax.fori_loop(0, count, step, 0, unroll=unroll)


def loop_carry(count, body, init, unroll=1):
    return lax.fori_loop(0, count, body, init, unroll=unroll)


def lane_block(ref, i, rows=None):
    window = pl.ds(pl.multiple_of(i * LANES, LANES), LANES)
    return ref[:, window] if rows is None else ref[rows, window]


PAD = 2
TURN = 16
BATCH = 4


def lane_part(x, i):
    return x[:, i * LANES : (i + 1) * LANES]


def row_part(x, i, size):
    return x[i * size : (i + 1) * size]


def spread_body(x_ref, out_ref, rows_ref):
    channels, blocks, _ = out_ref.shape

    def put(i):
        rows_ref[pl.ds(i * (channels + PAD), channels), :] = lane_block(x_ref, i).astype(F32)

    loop(blocks, put, 4)

    def take(c):
        out_ref[c] = rows_ref[pl.ds(c, blocks, stride=channels + PAD), :].astype(BF)

    loop(channels, take, 4)


def unpack_rows(x_ref, rows_ref, offset=0, blocks=None):
    items = x_ref.shape[0]
    blocks = blocks or x_ref.shape[1]

    def put(c):
        block = x_ref[c, offset : offset + blocks, :]
        rows_ref[pl.ds(c * (blocks + PAD), blocks), :] = block.astype(F32)

    loop(items, put, 16 if blocks <= TURN else 4)


def take_turn(rows_ref, out_ref):
    channels = out_ref.shape[0]

    def take(c):
        out_ref[c] = rows_ref[pl.ds(c, TURN, stride=channels + PAD), :].astype(BF)

    loop(channels, take, 8)


def put_pair(rows_ref, pair, x):
    channels = x.shape[0]
    pitch = channels + PAD
    for side in range(2):
        at = (2 * pair + side) * pitch
        rows_ref[at : at + channels, :] = lane_part(x, side)


def pair_window(pair):
    return slice(2 * pair * LANES, (2 * pair + 2) * LANES)


def values_body(wv_ref, tok_ref, out_ref, rows_ref):
    for p in range(TURN // 2):
        put_pair(rows_ref, p, dot(wv_ref[...], tok_ref[:, pair_window(p)]))
    take_turn(rows_ref, out_ref)


def grads_body(wg_ref, wo_ref, tok_ref, cot_ref, out_ref, rows_ref):
    for p in range(TURN // 2):
        gates = dot(wg_ref[...], tok_ref[:, pair_window(p)])
        put_pair(rows_ref, p, dot(wo_ref[...], cot_ref[:, pair_window(p)]) * gates)
    take_turn(rows_ref, out_ref)


def rotate(re, im, cos_part, sin_part):
    return re * cos_part - im * sin_part, re * sin_part + im * cos_part


def first_stage(rows_ref, m1_ref, tw_ref, mid_ref):
    count = m1_ref.shape[0]
    half = count // 2
    mid = F2 + PAD

    def step(j, turn):
        cos_part, sin_part = turn
        x = jnp.concatenate(
            [rows_ref[pl.ds(2 * j + side, count, stride=mid), :] for side in range(2)], axis=1
        )
        y = dot(m1_ref[...], x.astype(BF))
        re, im = rotate(y[:half], y[half:], cos_part, -sin_part)
        for side in range(2):
            mid_ref[pl.ds(2 * j + side, half, stride=2 * mid), :] = lane_part(re, side)
            mid_ref[pl.ds(mid + 2 * j + side, half, stride=2 * mid), :] = lane_part(im, side)
        return rotate(cos_part, sin_part, tw_ref[2], tw_ref[3])

    loop_carry(F2 // 2, step, (tw_ref[0], tw_ref[1]), 2)


def last_stage(rows_ref, m1_ref, tw_ref, mid_ref):
    count = m1_ref.shape[0]
    half = count // 2
    mid = F2 + PAD

    def step(j, turn):
        cos_part, sin_part = turn
        parts = []
        for part in range(2):
            sides = [
                mid_ref[pl.ds(part * mid + 2 * j + side, half, stride=2 * mid), :]
                for side in range(2)
            ]
            parts.append(jnp.concatenate(sides, axis=1))
        re, im = rotate(parts[0], parts[1], cos_part, sin_part)
        y = dot(m1_ref[...], jnp.concatenate([re, im], axis=0).astype(BF))
        for side in range(2):
            rows_ref[pl.ds(2 * j + side, count, stride=mid), :] = lane_part(y, side)
        return rotate(cos_part, sin_part, tw_ref[2], tw_ref[3])

    loop_carry(F2 // 2, step, (tw_ref[0], tw_ref[1]), 2)


def part_rows(k1, part):
    return pl.ds((2 * k1 + part) * (F2 + PAD), F2)


def to_spectrum(mid_ref, first, m2_ref, m3_ref, tw2_ref):
    stacked = []
    for p in range(BATCH // 2):
        pair = [
            jnp.concatenate([mid_ref[part_rows(k1, 0), :], mid_ref[part_rows(k1, 1), :]], axis=0)
            for k1 in (first + 2 * p, first + 2 * p + 1)
        ]
        y = dot(m2_ref[...], jnp.concatenate(pair, axis=1).astype(BF))
        re, im = rotate(y[:F2], y[F2:], tw2_ref[0], -tw2_ref[1])
        for side in range(2):
            stacked.append(
                jnp.concatenate([lane_part(re, side), lane_part(im, side)], axis=1).astype(BF)
            )
    return dot(jnp.concatenate(stacked, axis=0), m3_ref[...]).astype(BF)


def from_spectrum(mid_ref, first, blocks, m2_ref, m3_ref, tw2_ref):
    stacked = [jnp.concatenate(block, axis=1).astype(BF) for block in blocks]
    y = dot(jnp.concatenate(stacked, axis=0), m3_ref[...])
    for p in range(BATCH // 2):
        sides = [row_part(y, 2 * p + side, F2) for side in range(2)]
        re, im = rotate(
            jnp.concatenate([lane_part(s, 0) for s in sides], axis=1),
            jnp.concatenate([lane_part(s, 1) for s in sides], axis=1),
            tw2_ref[0],
            tw2_ref[1],
        )
        z = dot(m2_ref[...], jnp.concatenate([re, im], axis=0).astype(BF))
        for side in range(2):
            k1 = first + 2 * p + side
            mid_ref[part_rows(k1, 0), :] = lane_part(z[:F2], side)
            mid_ref[part_rows(k1, 1), :] = lane_part(z[F2:], side)


def split(spec):
    spec = spec.astype(F32)
    return spec[:, :F3], spec[:, F3:]


def kernel_parts(core_ref, own_ref, other_ref, k1):
    own, other = own_ref[k1].astype(F32), other_ref[k1].astype(F32)
    on_core_zero = core_ref[0] == 0
    return jnp.where(on_core_zero, own, other), jnp.where(on_core_zero, other, own)


def pack_rows(rows_ref, out_ref):
    items, blocks, _ = out_ref.shape

    def put(c):
        out_ref[c] = rows_ref[pl.ds(c * (blocks + PAD), blocks), :].astype(BF)

    loop(items, put, 4)


def values_transform_body(
    core_ref, z_ref, own_ref, other_ref, m1_ref, m2_ref, m3_ref, n1_ref, n2_ref, n3_ref,
    tw_ref, tw2_ref, out_ref, spec_ref, rows_ref, mid_ref,
):
    count = spec_ref.shape[0]
    unpack_rows(z_ref, rows_ref)
    first_stage(rows_ref, m1_ref, tw_ref, mid_ref)

    def spectrum(b):
        spec = to_spectrum(mid_ref, b * BATCH, m2_ref, m3_ref, tw2_ref)
        for t in range(BATCH):
            spec_ref[b * BATCH + t] = row_part(spec, t, F2)

    loop(count // BATCH, spectrum)

    def product(b):
        blocks = []
        for t in range(BATCH):
            k1 = b * BATCH + t
            kern_re, kern_im = kernel_parts(core_ref, own_ref, other_ref, k1)
            blocks.append(rotate(*split(spec_ref[k1]), kern_re, kern_im))
        from_spectrum(mid_ref, b * BATCH, blocks, n2_ref, n3_ref, tw2_ref)

    loop(count // BATCH, product)
    last_stage(rows_ref, n1_ref, tw_ref, mid_ref)
    pack_rows(rows_ref, out_ref)


def grads_transform_body(
    core_ref, z_ref, own_ref, other_ref, values_ref, m1_ref, m2_ref, m3_ref, n1_ref, n2_ref,
    n3_ref, tw_ref, tw2_ref, out_ref, keep_ref, send_ref, rows_ref, mid_ref, spec_ref,
):
    count = values_ref.shape[0]
    on_core_zero = core_ref[0] == 0
    unpack_rows(z_ref, rows_ref)
    first_stage(rows_ref, m1_ref, tw_ref, mid_ref)

    def spectrum(b):
        spec = to_spectrum(mid_ref, b * BATCH, m2_ref, m3_ref, tw2_ref)
        for t in range(BATCH):
            k1 = b * BATCH + t
            grad = row_part(spec, t, F2)
            spec_ref[k1] = grad
            value_re, value_im = split(values_ref[k1])
            re, im = rotate(*split(grad), value_re, -value_im)
            keep_ref[k1] = jnp.where(on_core_zero, re, im).astype(BF)
            send_ref[k1] = jnp.where(on_core_zero, im, re).astype(BF)

    loop(count // BATCH, spectrum)

    def product(b):
        blocks = []
        for t in range(BATCH):
            k1 = b * BATCH + t
            kern_re, kern_im = kernel_parts(core_ref, own_ref, other_ref, k1)
            blocks.append(rotate(*split(spec_ref[k1]), kern_re, -kern_im))
        from_spectrum(mid_ref, b * BATCH, blocks, n2_ref, n3_ref, tw2_ref)

    loop(count // BATCH, product)
    last_stage(rows_ref, n1_ref, tw_ref, mid_ref)
    pack_rows(rows_ref, out_ref)


def hermitian(ref, sign, flip_rows_ref, flip_lanes_ref, store):
    count = ref.shape[0]
    flip_rows_ref[...] = flip_matrix(BATCH * F2, 1)
    flip_lanes_ref[...] = flip_matrix(F3, 1)
    head = ref[0]
    head_rows = flip_matrix(F2, 0)
    turned = dot(head_rows, dot(head, flip_lanes_ref[...]).astype(BF))
    first = dot(head_rows, dot(head, flip_matrix(F3, 0)).astype(BF))
    row = lax.broadcasted_iota(jnp.int32, turned.shape, 0)
    store(0, 0.5 * (head.astype(F32) + sign * jnp.where(row == 0, first, turned)))

    def batch(b, keep=BATCH):
        low = count - BATCH - b * BATCH
        rows = jnp.concatenate([ref[low + t] for t in range(BATCH)], axis=0)
        turned = dot(flip_rows_ref[...], dot(rows, flip_lanes_ref[...]).astype(BF))
        for t in range(keep):
            k1 = b * BATCH + 1 + t
            store(k1, 0.5 * (ref[k1].astype(F32) + sign * row_part(turned, t, F2)))

    loop(count // BATCH - 1, batch)
    batch(count // BATCH - 1, BATCH - 1)


def terms_body(
    core_ref, keep_ref, recv_ref, out_ref, sum_ref, flip_rows_ref, flip_lanes_ref
):
    sign = jnp.where(core_ref[0] == 0, 1.0, -1.0)

    def add(k1):
        sum_ref[k1] = (keep_ref[k1].astype(F32) + recv_ref[k1].astype(F32)).astype(BF)

    loop(keep_ref.shape[0], add, 4)

    def store(k1, block):
        out_ref[k1] = block.astype(BF)

    hermitian(sum_ref, sign, flip_rows_ref, flip_lanes_ref, store)


def slot(place_ref, index, size, axes=3):
    at = 0
    for axis in range(3 - axes, 3):
        digit = lax.rem(lax.div(index, size ** (2 - axis)), size)
        at = at * size + lax.rem(place_ref[1 + axis] - digit + size, size)
    return at


def response_body(
    size, place_ref, got_ref, out_ref, own_ref, flip_rows_ref, flip_lanes_ref
):
    sign = jnp.where(place_ref[0] == 0, 1.0, -1.0)

    def order(k1):
        own_ref[k1] = got_ref[slot(place_ref, k1, size)]

    loop(own_ref.shape[0], order, 4)

    def store(k1, block):
        out_ref[k1] = block.astype(BF)

    hermitian(own_ref, sign, flip_rows_ref, flip_lanes_ref, store)


def gather_pair(rows_ref, pair, channels):
    return jnp.concatenate(
        [rows_ref[pl.ds(2 * pair + side, channels, stride=TURN + PAD), :] for side in range(2)],
        axis=1,
    )


def gates_body(
    wv_ref, wg_ref, wo_ref, wpg_ref, skip_ref, tok_ref, cot_ref, conv_ref,
    part_ref, own_ref, rows_ref,
):
    channels = conv_ref.shape[0]
    unpack_rows(conv_ref, rows_ref)
    for p in range(TURN // 2):
        window = pair_window(p)
        tok = tok_ref[:, window]
        values = dot(wv_ref[...], tok).astype(BF).astype(F32)
        hidden = dot(wo_ref[...], cot_ref[:, window])
        own = (hidden * dot(wg_ref[...], tok)).astype(BF).astype(F32)
        mixed = gather_pair(rows_ref, p, channels) + skip_ref[...] * values
        part_ref[:, window] = dot(wpg_ref[...], (hidden * mixed).astype(BF))
        own_ref[:, window] = skip_ref[...] * own


def final_body(wpv_ref, part_ref, own_ref, back_ref, out_ref, rows_ref):
    channels = back_ref.shape[0]
    unpack_rows(back_ref, rows_ref)
    for p in range(TURN // 2):
        window = pair_window(p)
        grad = gather_pair(rows_ref, p, channels) + own_ref[:, window]
        out_ref[:, window] = (part_ref[:, window] + dot(wpv_ref[...], grad.astype(BF))).astype(BF)


def chunked(body, micros, small, chunks, outs, messages=(), scratch=()):
    steps = chunks[0].shape[1] // (TURN * LANES)
    whole = [pl.BlockSpec(a.shape, lambda i: (0, 0)) for a in small]
    wide = lambda a: pl.BlockSpec((a.shape[0], TURN * LANES), lambda i: (0, i))
    turn = lambda a: pl.BlockSpec((a.shape[0], TURN, LANES), lambda i: (0, i, 0))
    spec = lambda a: wide(a) if len(a.shape) == 2 else turn(a)
    return pl.pallas_call(
        body,
        grid=(steps,),
        out_shape=outs,
        in_specs=whole + [spec(a) for a in chunks + tuple(messages)],
        out_specs=[spec(a) for a in outs],
        scratch_shapes=list(scratch),
        compiler_params=pltpu.CompilerParams(vmem_limit_bytes=32 << 20),
        cost_estimate=cost(micros),
    )(*small, *(in_hbm(a) for a in chunks + tuple(messages)))


def in_hbm(a):
    return pltpu.with_memory_space_constraint(a, pltpu.HBM)


def kernel_grad_body(size, place_ref, keep_ref, recv_ref, out_ref, rows_ref):
    channels, blocks, _ = keep_ref.shape
    core = place_ref[0]
    for ref, part in ((keep_ref, core), (recv_ref, 1 - core)):

        def put(c, ref=ref):
            at = lax.div(c, size * size) * size * size + slot(place_ref, c, size, 2)
            rows_ref[pl.ds(c * (blocks + PAD), blocks), :] = ref[at].astype(F32)

        loop(channels, put, 4)

        def step(i, part=part):
            window = pl.ds(pl.multiple_of(i * LANES, LANES), LANES)
            rows = rows_ref[pl.ds(i, channels, stride=blocks + PAD), :]
            out_ref[part, :, window] = rows.astype(BF)

        loop(blocks, step, 4)


SWAP = [(0, 1), (1, 0)]
RING = ("zh", "y", "x")
SEQ = RING
GROUP = ("zl",) + RING


def ring_step(y, axis, size):
    me = lax.axis_index(RING[axis])
    parts = []
    for step in range(size):
        slab = lax.dynamic_slice_in_dim(y, lax.rem(me + step, size), 1, axis)
        ring = [(i, (i + step) % size) for i in range(size)]
        parts.append(lax.ppermute(slab, RING[axis], ring) if step else slab)
    return jnp.concatenate(parts, axis=axis)


def cube(x, size):
    return x.reshape((size, size, size) + x.shape[1:])


def exchange(x):
    return lax.all_to_all(x, GROUP, split_axis=0, concat_axis=0, tiled=True)


def per_device(tokens, kernel, skip, w_proj, w_out, cotangent):
    size = lax.axis_size("x")
    first_len = size**3
    core = lax.axis_index("core")
    z_low = lax.axis_index("zl")
    channels, positions = tokens.shape[1:]
    whole = first_len * positions
    place = jnp.stack([core] + [lax.axis_index(name) for name in RING]).astype(jnp.int32)
    tok = tokens.reshape(channels, positions)
    cot = cotangent.reshape(channels, positions)
    blocks = positions // LANES
    shaped = jax.ShapeDtypeStruct

    bf = functools.partial(jnp.asarray, dtype=BF)
    skip_full = jnp.broadcast_to(skip[:, None], (channels, 2 * LANES))
    m1, n1 = bf(dft_blocks(first_len, -1.0)), bf(dft_blocks(first_len, 1.0))
    m2, n2 = bf(dft_blocks(F2, -1.0)), bf(dft_blocks(F2, 1.0))
    m3, n3 = bf(dft_blocks(F3, -1.0).T), bf(dft_blocks(F3, 1.0).T)
    freq = np.arange(first_len)[:, None]
    pair = np.arange(2 * F3)[None, :]
    tw = jnp.asarray(
        np.concatenate(
            [turns(freq * pair, whole), turns(freq * np.full_like(pair, 2 * F3), whole)]
        )
    )
    tw2 = turns(np.arange(F2)[:, None] * np.arange(F3)[None, :], F2 * F3)
    tw2 = jnp.asarray(np.concatenate([tw2, tw2], axis=2))
    share = first_len
    half = share // 2
    mid_rows = pltpu.VMEM((2 * first_len * (F2 + PAD), F3), F32)
    turn_rows = pltpu.VMEM((TURN * (channels + PAD), LANES), F32)
    turn_items = pltpu.VMEM((channels * (TURN + PAD), LANES), F32)
    part = shaped((share, blocks, LANES), BF)
    flip_scratch = [
        pltpu.VMEM((first_len, F2, F3), BF),
        pltpu.VMEM((BATCH * F2, BATCH * F2), BF),
        pltpu.VMEM((F3, F3), BF),
    ]
    message = pltpu.HBM((channels, blocks, LANES), BF)
    spectrum = shaped((first_len, F2, 2 * F3), BF)
    wv, wg = w_proj[:, :channels].T, w_proj[:, channels:].T
    wpv, wpg = w_proj[:, :channels], w_proj[:, channels:]

    chosen = lax.dynamic_slice(kernel, (core, z_low * share, 0), (1, share, positions))[0]
    response = call(
        spread_body, part, [pltpu.VMEM((blocks * (share + PAD), LANES), F32)],
        chosen, micros=3,
    )
    response = ring_step(cube(response, size), 0, size)

    (values,) = chunked(values_body, 5, (wv,), (tok,), (message,), (), (turn_rows,))
    values = exchange(values)
    (grads,) = chunked(grads_body, 6, (wg, w_out), (tok, cot), (message,), (), (turn_rows,))
    grads, response = lax.optimization_barrier((grads, response))
    response = ring_step(ring_step(response, 1, size), 2, size)
    grads, values = lax.optimization_barrier((grads, values))
    grads = exchange(grads)
    response = call(
        functools.partial(response_body, size), part, flip_scratch,
        place, response.reshape(part.shape),
        smem=1, micros=4,
    )
    other = lax.ppermute(response, "core", SWAP)
    tables = (m1, m2, m3, n1, n2, n3, tw, tw2)
    conv, spec = call(
        values_transform_body, (message, spectrum), [mid_rows, mid_rows],
        place, values, response, other, *tables,
        smem=1, micros=20,
    )
    conv, grads = lax.optimization_barrier((conv, grads))
    conv = exchange(conv)
    back, keep, send = call(
        grads_transform_body, (message, part, part),
        [mid_rows, mid_rows, pltpu.VMEM((first_len, F2, 2 * F3), BF)],
        place, grads, response, other, spec, *tables,
        smem=1, micros=22,
    )
    terms = call(
        terms_body, part, flip_scratch,
        place, keep, lax.ppermute(send, "core", SWAP),
        smem=1, micros=5,
    )
    terms = ring_step(cube(terms, size), 0, size)
    back, conv = lax.optimization_barrier((back, conv))
    back = exchange(back)
    gates, own = chunked(
        gates_body, 10, (wv, wg, w_out, wpg, skip_full), (tok, cot),
        (pltpu.HBM((channels, positions), F32),) * 2, (conv,), (turn_items,),
    )
    terms = ring_step(ring_step(terms, 1, size), 2, size)
    me = lax.axis_index(RING[0])

    def halves(of_core):
        slabs = [
            lax.dynamic_slice_in_dim(terms, lax.rem(me - of_core * (size // 2) - i + size, size), 1, 0)
            for i in range(size // 2)
        ]
        return jnp.concatenate(slabs, axis=0).reshape(half, blocks, LANES)

    kernel_grad = call(
        functools.partial(kernel_grad_body, size),
        shaped((2, half, positions), BF),
        [pltpu.VMEM((half * (blocks + PAD), LANES), F32)],
        place, halves(core), lax.ppermute(halves(1 - core), "core", SWAP),
        smem=1, micros=3,
    )
    (input_grad,) = chunked(
        final_body, 6, (wpv,), (gates, own),
        (pltpu.HBM((channels, positions), BF),), (back,), (turn_items,),
    )
    return input_grad.reshape(1, channels, positions), kernel_grad


def solution(mesh):
    sequences, groups = mesh.devices.shape
    size = round(groups ** (1 / 3))
    fine = Mesh(
        mesh.devices.reshape(2, sequences // 2, size, size, size), ("zl", "core") + RING
    )
    dp = ("zl", "core")
    signal = P(dp, None, SEQ)
    return jax.shard_map(
        per_device,
        mesh=fine,
        in_specs=(signal, P(None, None, SEQ), P(), P(), P(), signal),
        out_specs=(signal, P(None, dp, SEQ)),
        check_vma=False,
    )
```

```python
import functools
import math

import jax
import jax.numpy as jnp
import numpy as np
from jax import lax
from jax.experimental import pallas as pl
from jax.experimental.pallas import tpu as pltpu
from jax.sharding import Mesh, PartitionSpec as P


BF = jnp.bfloat16
F32 = jnp.float32
F2 = 64
F3 = 128
LANES = 128


def dft_blocks(length, direction):
    ids = np.arange(length)
    angles = (ids[:, None] * ids[None, :] % length).astype(np.float32) * np.float32(
        2.0 * math.pi / length
    )
    scale = np.float32(1.0 / math.sqrt(length))
    real = np.cos(angles) * scale
    imag = direction * np.sin(angles) * scale
    return np.block([[real, -imag], [imag, real]]).astype(np.float32)


def turns(ids, modulus):
    angles = (ids % modulus).astype(np.float64) * (2.0 * math.pi / modulus)
    return np.stack([np.cos(angles), np.sin(angles)]).astype(np.float32)


def flip_matrix(size, shift):
    row = lax.broadcasted_iota(jnp.int32, (size, size), 0)
    column = lax.broadcasted_iota(jnp.int32, (size, size), 1)
    total = row + column
    hit = total == size - shift
    if not shift:
        hit = jnp.logical_or(hit, total == 0)
    return jnp.where(hit, 1.0, 0.0).astype(BF)


def vmem_specs(count):
    return [pl.BlockSpec(memory_space=pltpu.VMEM)] * count


SMEM_SPEC = pl.BlockSpec(memory_space=pltpu.SMEM)


def call(body, out_shape, scratch, *args, smem=0, micros=20):
    multi = isinstance(out_shape, (tuple, list))
    return pl.pallas_call(
        body,
        out_shape=out_shape,
        in_specs=[SMEM_SPEC] * smem + vmem_specs(len(args) - smem),
        out_specs=vmem_specs(len(out_shape)) if multi else vmem_specs(1)[0],
        scratch_shapes=scratch,
        compiler_params=pltpu.CompilerParams(vmem_limit_bytes=48 << 20),
        cost_estimate=cost(micros),
    )(*args)


def cost(micros):
    return pl.CostEstimate(
        flops=micros * 10**9, transcendentals=0, bytes_accessed=micros * 3 * 10**6
    )


def dot(a, b):
    return jnp.dot(a, b, preferred_element_type=F32)


def loop(count, body, unroll=1):
    def step(i, carry):
        body(i)
        return carry

    lax.fori_loop(0, count, step, 0, unroll=unroll)


def loop_carry(count, body, init, unroll=1):
    return lax.fori_loop(0, count, body, init, unroll=unroll)


def lane_block(ref, i, rows=None):
    window = pl.ds(pl.multiple_of(i * LANES, LANES), LANES)
    return ref[:, window] if rows is None else ref[rows, window]


PAD = 2
TURN = 16
BATCH = 4


def lane_part(x, i):
    return x[:, i * LANES : (i + 1) * LANES]


def row_part(x, i, size):
    return x[i * size : (i + 1) * size]


def spread_body(x_ref, out_ref, rows_ref):
    channels, blocks, _ = out_ref.shape

    def put(i):
        rows_ref[pl.ds(i * (channels + PAD), channels), :] = lane_block(x_ref, i).astype(F32)

    loop(blocks, put, 4)

    def take(c):
        out_ref[c] = rows_ref[pl.ds(c, blocks, stride=channels + PAD), :].astype(BF)

    loop(channels, take, 4)


def spread_call(kernel, at, share):
    positions = kernel.shape[2]
    blocks = positions // LANES
    return pl.pallas_call(
        lambda at_ref, x_ref, out_ref, rows_ref: spread_body(x_ref.at[0], out_ref, rows_ref),
        grid_spec=pltpu.PrefetchScalarGridSpec(
            num_scalar_prefetch=1,
            grid=(1,),
            in_specs=[pl.BlockSpec((1, share, positions), lambda i, at: (at[0], at[1], 0))],
            out_specs=pl.BlockSpec((share, blocks, LANES), lambda i, at: (0, 0, 0)),
            scratch_shapes=[pltpu.VMEM((blocks * (share + PAD), LANES), F32)],
        ),
        out_shape=jax.ShapeDtypeStruct((share, blocks, LANES), BF),
        compiler_params=pltpu.CompilerParams(vmem_limit_bytes=32 << 20),
        cost_estimate=cost(3),
        name="spread",
    )(at, in_hbm(kernel))


def unpack_rows(x_ref, rows_ref, offset=0, blocks=None):
    items = x_ref.shape[0]
    blocks = blocks or x_ref.shape[1]

    def put(c):
        block = x_ref[c, offset : offset + blocks, :]
        rows_ref[pl.ds(c * (blocks + PAD), blocks), :] = block.astype(F32)

    loop(items, put, 16 if blocks <= TURN else 4)


def take_turn(rows_ref, out_ref):
    channels = out_ref.shape[0]

    def take(c):
        out_ref[c] = rows_ref[pl.ds(c, TURN, stride=channels + PAD), :].astype(BF)

    loop(channels, take, 8)


def put_pair(rows_ref, pair, x):
    channels = x.shape[0]
    pitch = channels + PAD
    for side in range(2):
        at = (2 * pair + side) * pitch
        rows_ref[at : at + channels, :] = lane_part(x, side)


def pair_window(pair):
    return slice(2 * pair * LANES, (2 * pair + 2) * LANES)


def values_body(wv_ref, tok_ref, out_ref, rows_ref):
    for p in range(TURN // 2):
        put_pair(rows_ref, p, dot(wv_ref[...], tok_ref[:, pair_window(p)]))
    take_turn(rows_ref, out_ref)


def grads_body(wg_ref, wo_ref, tok_ref, cot_ref, out_ref, rows_ref):
    for p in range(TURN // 2):
        gates = dot(wg_ref[...], tok_ref[:, pair_window(p)])
        put_pair(rows_ref, p, dot(wo_ref[...], cot_ref[:, pair_window(p)]) * gates)
    take_turn(rows_ref, out_ref)


def rotate(re, im, cos_part, sin_part):
    return re * cos_part - im * sin_part, re * sin_part + im * cos_part


def first_stage(rows_ref, m1_ref, tw_ref, mid_ref):
    count = m1_ref.shape[0]
    half = count // 2
    mid = F2 + PAD

    def step(j, turn):
        cos_part, sin_part = turn
        x = jnp.concatenate(
            [rows_ref[pl.ds(2 * j + side, count, stride=mid), :] for side in range(2)], axis=1
        )
        y = dot(m1_ref[...], x.astype(BF))
        re, im = rotate(y[:half], y[half:], cos_part, -sin_part)
        for side in range(2):
            mid_ref[pl.ds(2 * j + side, half, stride=2 * mid), :] = lane_part(re, side)
            mid_ref[pl.ds(mid + 2 * j + side, half, stride=2 * mid), :] = lane_part(im, side)
        return rotate(cos_part, sin_part, tw_ref[2], tw_ref[3])

    loop_carry(F2 // 2, step, (tw_ref[0], tw_ref[1]), 2)


def last_stage(rows_ref, m1_ref, tw_ref, mid_ref):
    count = m1_ref.shape[0]
    half = count // 2
    mid = F2 + PAD

    def step(j, turn):
        cos_part, sin_part = turn
        parts = []
        for part in range(2):
            sides = [
                mid_ref[pl.ds(part * mid + 2 * j + side, half, stride=2 * mid), :]
                for side in range(2)
            ]
            parts.append(jnp.concatenate(sides, axis=1))
        re, im = rotate(parts[0], parts[1], cos_part, sin_part)
        y = dot(m1_ref[...], jnp.concatenate([re, im], axis=0).astype(BF))
        for side in range(2):
            rows_ref[pl.ds(2 * j + side, count, stride=mid), :] = lane_part(y, side)
        return rotate(cos_part, sin_part, tw_ref[2], tw_ref[3])

    loop_carry(F2 // 2, step, (tw_ref[0], tw_ref[1]), 2)


def part_rows(k1, part):
    return pl.ds((2 * k1 + part) * (F2 + PAD), F2)


def to_spectrum(mid_ref, first, m2_ref, m3_ref, tw2_ref):
    stacked = []
    for p in range(BATCH // 2):
        pair = [
            jnp.concatenate([mid_ref[part_rows(k1, 0), :], mid_ref[part_rows(k1, 1), :]], axis=0)
            for k1 in (first + 2 * p, first + 2 * p + 1)
        ]
        y = dot(m2_ref[...], jnp.concatenate(pair, axis=1).astype(BF))
        re, im = rotate(y[:F2], y[F2:], tw2_ref[0], -tw2_ref[1])
        for side in range(2):
            stacked.append(
                jnp.concatenate([lane_part(re, side), lane_part(im, side)], axis=1).astype(BF)
            )
    return dot(jnp.concatenate(stacked, axis=0), m3_ref[...]).astype(BF)


def from_spectrum(mid_ref, first, blocks, m2_ref, m3_ref, tw2_ref):
    stacked = [jnp.concatenate(block, axis=1).astype(BF) for block in blocks]
    y = dot(jnp.concatenate(stacked, axis=0), m3_ref[...])
    for p in range(BATCH // 2):
        sides = [row_part(y, 2 * p + side, F2) for side in range(2)]
        re, im = rotate(
            jnp.concatenate([lane_part(s, 0) for s in sides], axis=1),
            jnp.concatenate([lane_part(s, 1) for s in sides], axis=1),
            tw2_ref[0],
            tw2_ref[1],
        )
        z = dot(m2_ref[...], jnp.concatenate([re, im], axis=0).astype(BF))
        for side in range(2):
            k1 = first + 2 * p + side
            mid_ref[part_rows(k1, 0), :] = lane_part(z[:F2], side)
            mid_ref[part_rows(k1, 1), :] = lane_part(z[F2:], side)


def split(spec):
    spec = spec.astype(F32)
    return spec[:, :F3], spec[:, F3:]


def kernel_parts(core_ref, own_ref, other_ref, k1):
    own, other = own_ref[k1].astype(F32), other_ref[k1].astype(F32)
    on_core_zero = core_ref[0] == 0
    return jnp.where(on_core_zero, own, other), jnp.where(on_core_zero, other, own)


def pack_rows(rows_ref, out_ref):
    items, blocks, _ = out_ref.shape

    def put(c):
        out_ref[c] = rows_ref[pl.ds(c * (blocks + PAD), blocks), :].astype(BF)

    loop(items, put, 4)


def values_transform_body(
    core_ref, z_ref, own_ref, other_ref, m1_ref, m2_ref, m3_ref, n1_ref, n2_ref, n3_ref,
    tw_ref, tw2_ref, out_ref, spec_ref, rows_ref, mid_ref,
):
    count = spec_ref.shape[0]
    unpack_rows(z_ref, rows_ref)
    first_stage(rows_ref, m1_ref, tw_ref, mid_ref)

    def spectrum(b):
        spec = to_spectrum(mid_ref, b * BATCH, m2_ref, m3_ref, tw2_ref)
        for t in range(BATCH):
            spec_ref[b * BATCH + t] = row_part(spec, t, F2)

    loop(count // BATCH, spectrum)

    def product(b):
        blocks = []
        for t in range(BATCH):
            k1 = b * BATCH + t
            kern_re, kern_im = kernel_parts(core_ref, own_ref, other_ref, k1)
            blocks.append(rotate(*split(spec_ref[k1]), kern_re, kern_im))
        from_spectrum(mid_ref, b * BATCH, blocks, n2_ref, n3_ref, tw2_ref)

    loop(count // BATCH, product)
    last_stage(rows_ref, n1_ref, tw_ref, mid_ref)
    pack_rows(rows_ref, out_ref)


def grads_transform_body(
    core_ref, z_ref, own_ref, other_ref, values_ref, m1_ref, m2_ref, m3_ref, n1_ref, n2_ref,
    n3_ref, tw_ref, tw2_ref, out_ref, keep_ref, send_ref, rows_ref, mid_ref, spec_ref,
):
    count = values_ref.shape[0]
    on_core_zero = core_ref[0] == 0
    unpack_rows(z_ref, rows_ref)
    first_stage(rows_ref, m1_ref, tw_ref, mid_ref)

    def spectrum(b):
        spec = to_spectrum(mid_ref, b * BATCH, m2_ref, m3_ref, tw2_ref)
        for t in range(BATCH):
            k1 = b * BATCH + t
            grad = row_part(spec, t, F2)
            spec_ref[k1] = grad
            value_re, value_im = split(values_ref[k1])
            re, im = rotate(*split(grad), value_re, -value_im)
            keep_ref[k1] = jnp.where(on_core_zero, re, im).astype(BF)
            send_ref[k1] = jnp.where(on_core_zero, im, re).astype(BF)

    loop(count // BATCH, spectrum)

    def product(b):
        blocks = []
        for t in range(BATCH):
            k1 = b * BATCH + t
            kern_re, kern_im = kernel_parts(core_ref, own_ref, other_ref, k1)
            blocks.append(rotate(*split(spec_ref[k1]), kern_re, -kern_im))
        from_spectrum(mid_ref, b * BATCH, blocks, n2_ref, n3_ref, tw2_ref)

    loop(count // BATCH, product)
    last_stage(rows_ref, n1_ref, tw_ref, mid_ref)
    pack_rows(rows_ref, out_ref)


def hermitian(ref, sign, flip_rows_ref, flip_lanes_ref, store):
    count = ref.shape[0]
    flip_rows_ref[...] = flip_matrix(BATCH * F2, 1)
    flip_lanes_ref[...] = flip_matrix(F3, 1)
    head = ref[0]
    head_rows = flip_matrix(F2, 0)
    turned = dot(head_rows, dot(head, flip_lanes_ref[...]).astype(BF))
    first = dot(head_rows, dot(head, flip_matrix(F3, 0)).astype(BF))
    row = lax.broadcasted_iota(jnp.int32, turned.shape, 0)
    store(0, 0.5 * (head.astype(F32) + sign * jnp.where(row == 0, first, turned)))

    def batch(b, keep=BATCH):
        low = count - BATCH - b * BATCH
        rows = jnp.concatenate([ref[low + t] for t in range(BATCH)], axis=0)
        turned = dot(flip_rows_ref[...], dot(rows, flip_lanes_ref[...]).astype(BF))
        for t in range(keep):
            k1 = b * BATCH + 1 + t
            store(k1, 0.5 * (ref[k1].astype(F32) + sign * row_part(turned, t, F2)))

    loop(count // BATCH - 1, batch)
    batch(count // BATCH - 1, BATCH - 1)


def terms_body(
    core_ref, keep_ref, recv_ref, out_ref, sum_ref, flip_rows_ref, flip_lanes_ref
):
    sign = jnp.where(core_ref[0] == 0, 1.0, -1.0)

    def add(k1):
        sum_ref[k1] = (keep_ref[k1].astype(F32) + recv_ref[k1].astype(F32)).astype(BF)

    loop(keep_ref.shape[0], add, 4)

    def store(k1, block):
        out_ref[k1] = block.astype(BF)

    hermitian(sum_ref, sign, flip_rows_ref, flip_lanes_ref, store)


def slot(place_ref, index, size, axes=3):
    at = 0
    for axis in range(3 - axes, 3):
        digit = lax.rem(lax.div(index, size ** (2 - axis)), size)
        at = at * size + lax.rem(place_ref[1 + axis] - digit + size, size)
    return at


def response_body(
    size, place_ref, got_ref, out_ref, own_ref, flip_rows_ref, flip_lanes_ref
):
    sign = jnp.where(place_ref[0] == 0, 1.0, -1.0)

    def order(k1):
        own_ref[k1] = got_ref[slot(place_ref, k1, size)]

    loop(own_ref.shape[0], order, 4)

    def store(k1, block):
        out_ref[k1] = block.astype(BF)

    hermitian(own_ref, sign, flip_rows_ref, flip_lanes_ref, store)


def gather_pair(rows_ref, pair, channels):
    return jnp.concatenate(
        [rows_ref[pl.ds(2 * pair + side, channels, stride=TURN + PAD), :] for side in range(2)],
        axis=1,
    )


def gates_body(
    wv_ref, wg_ref, wo_ref, wpg_ref, skip_ref, tok_ref, cot_ref, conv_ref,
    part_ref, own_ref, rows_ref,
):
    channels = conv_ref.shape[0]
    unpack_rows(conv_ref, rows_ref)
    for p in range(TURN // 2):
        window = pair_window(p)
        tok = tok_ref[:, window]
        values = dot(wv_ref[...], tok).astype(BF).astype(F32)
        hidden = dot(wo_ref[...], cot_ref[:, window])
        own = (hidden * dot(wg_ref[...], tok)).astype(BF).astype(F32)
        mixed = gather_pair(rows_ref, p, channels) + skip_ref[...] * values
        part_ref[:, window] = dot(wpg_ref[...], (hidden * mixed).astype(BF))
        own_ref[:, window] = skip_ref[...] * own


def final_body(wpv_ref, part_ref, own_ref, back_ref, out_ref, rows_ref):
    channels = back_ref.shape[0]
    unpack_rows(back_ref, rows_ref)
    for p in range(TURN // 2):
        window = pair_window(p)
        grad = gather_pair(rows_ref, p, channels) + own_ref[:, window]
        out_ref[:, window] = (part_ref[:, window] + dot(wpv_ref[...], grad.astype(BF))).astype(BF)


def chunked(body, micros, small, chunks, outs, messages=(), scratch=()):
    steps = chunks[0].shape[1] // (TURN * LANES)
    whole = [pl.BlockSpec(a.shape, lambda i: (0, 0)) for a in small]
    wide = lambda a: pl.BlockSpec((a.shape[0], TURN * LANES), lambda i: (0, i))
    turn = lambda a: pl.BlockSpec((a.shape[0], TURN, LANES), lambda i: (0, i, 0))
    spec = lambda a: wide(a) if len(a.shape) == 2 else turn(a)
    return pl.pallas_call(
        body,
        grid=(steps,),
        out_shape=outs,
        in_specs=whole + [spec(a) for a in chunks + tuple(messages)],
        out_specs=[spec(a) for a in outs],
        scratch_shapes=list(scratch),
        compiler_params=pltpu.CompilerParams(vmem_limit_bytes=32 << 20),
        cost_estimate=cost(micros),
    )(*small, *(in_hbm(a) for a in chunks + tuple(messages)))


def in_hbm(a):
    return pltpu.with_memory_space_constraint(a, pltpu.HBM)


def kernel_grad_body(size, place_ref, keep_ref, recv_ref, out_ref, rows_ref):
    channels, blocks, _ = keep_ref.shape
    core = place_ref[0]
    for ref, part in ((keep_ref, core), (recv_ref, 1 - core)):

        def put(c, ref=ref):
            at = lax.div(c, size * size) * size * size + slot(place_ref, c, size, 2)
            rows_ref[pl.ds(c * (blocks + PAD), blocks), :] = ref[at].astype(F32)

        loop(channels, put, 4)

        def step(i, part=part):
            window = pl.ds(pl.multiple_of(i * LANES, LANES), LANES)
            rows = rows_ref[pl.ds(i, channels, stride=blocks + PAD), :]
            out_ref[part, :, window] = rows.astype(BF)

        loop(blocks, step, 4)


SWAP = [(0, 1), (1, 0)]
RING = ("zh", "y", "x")
SEQ = RING
GROUP = ("zl",) + RING


def ring_step(y, axis, size):
    me = lax.axis_index(RING[axis])
    parts = []
    for step in range(size):
        slab = lax.dynamic_slice_in_dim(y, lax.rem(me + step, size), 1, axis)
        ring = [(i, (i + step) % size) for i in range(size)]
        parts.append(lax.ppermute(slab, RING[axis], ring) if step else slab)
    return jnp.concatenate(parts, axis=axis)


def cube(x, size):
    return x.reshape((size, size, size) + x.shape[1:])


def exchange(x):
    return lax.all_to_all(x, GROUP, split_axis=0, concat_axis=0, tiled=True)


def per_device(tokens, kernel, skip, w_proj, w_out, cotangent):
    size = lax.axis_size("x")
    first_len = size**3
    core = lax.axis_index("core")
    z_low = lax.axis_index("zl")
    channels, positions = tokens.shape[1:]
    whole = first_len * positions
    place = jnp.stack([core] + [lax.axis_index(name) for name in RING]).astype(jnp.int32)
    tok = tokens.reshape(channels, positions)
    cot = cotangent.reshape(channels, positions)
    blocks = positions // LANES
    shaped = jax.ShapeDtypeStruct

    bf = functools.partial(jnp.asarray, dtype=BF)
    skip_full = jnp.broadcast_to(skip[:, None], (channels, 2 * LANES))
    m1, n1 = bf(dft_blocks(first_len, -1.0)), bf(dft_blocks(first_len, 1.0))
    m2, n2 = bf(dft_blocks(F2, -1.0)), bf(dft_blocks(F2, 1.0))
    m3, n3 = bf(dft_blocks(F3, -1.0).T), bf(dft_blocks(F3, 1.0).T)
    freq = np.arange(first_len)[:, None]
    pair = np.arange(2 * F3)[None, :]
    tw = jnp.asarray(
        np.concatenate(
            [turns(freq * pair, whole), turns(freq * np.full_like(pair, 2 * F3), whole)]
        )
    )
    tw2 = turns(np.arange(F2)[:, None] * np.arange(F3)[None, :], F2 * F3)
    tw2 = jnp.asarray(np.concatenate([tw2, tw2], axis=2))
    share = first_len
    half = share // 2
    mid_rows = pltpu.VMEM((2 * first_len * (F2 + PAD), F3), F32)
    turn_rows = pltpu.VMEM((TURN * (channels + PAD), LANES), F32)
    turn_items = pltpu.VMEM((channels * (TURN + PAD), LANES), F32)
    part = shaped((share, blocks, LANES), BF)
    flip_scratch = [
        pltpu.VMEM((first_len, F2, F3), BF),
        pltpu.VMEM((BATCH * F2, BATCH * F2), BF),
        pltpu.VMEM((F3, F3), BF),
    ]
    message = pltpu.HBM((channels, blocks, LANES), BF)
    spectrum = shaped((first_len, F2, 2 * F3), BF)
    wv, wg = w_proj[:, :channels].T, w_proj[:, channels:].T
    wpv, wpg = w_proj[:, :channels], w_proj[:, channels:]

    response = spread_call(kernel, jnp.stack([core, z_low]).astype(jnp.int32), share)
    response = ring_step(cube(response, size), 0, size)

    (values,) = chunked(values_body, 5, (wv,), (tok,), (message,), (), (turn_rows,))
    values = exchange(values)
    (grads,) = chunked(grads_body, 6, (wg, w_out), (tok, cot), (message,), (), (turn_rows,))
    grads, response = lax.optimization_barrier((grads, response))
    response = ring_step(ring_step(response, 1, size), 2, size)
    grads, values = lax.optimization_barrier((grads, values))
    grads = exchange(grads)
    response = call(
        functools.partial(response_body, size), part, flip_scratch,
        place, response.reshape(part.shape),
        smem=1, micros=4,
    )
    other = lax.ppermute(response, "core", SWAP)
    tables = (m1, m2, m3, n1, n2, n3, tw, tw2)
    conv, spec = call(
        values_transform_body, (message, spectrum), [mid_rows, mid_rows],
        place, values, response, other, *tables,
        smem=1, micros=20,
    )
    conv, grads = lax.optimization_barrier((conv, grads))
    conv = exchange(conv)
    back, keep, send = call(
        grads_transform_body, (message, part, part),
        [mid_rows, mid_rows, pltpu.VMEM((first_len, F2, 2 * F3), BF)],
        place, grads, response, other, spec, *tables,
        smem=1, micros=22,
    )
    terms = call(
        terms_body, part, flip_scratch,
        place, keep, lax.ppermute(send, "core", SWAP),
        smem=1, micros=5,
    )
    terms = ring_step(cube(terms, size), 0, size)
    back, conv = lax.optimization_barrier((back, conv))
    back = exchange(back)
    gates, own = chunked(
        gates_body, 10, (wv, wg, w_out, wpg, skip_full), (tok, cot),
        (pltpu.HBM((channels, positions), F32),) * 2, (conv,), (turn_items,),
    )
    terms = ring_step(ring_step(terms, 1, size), 2, size)
    me = lax.axis_index(RING[0])

    def halves(of_core):
        slabs = [
            lax.dynamic_slice_in_dim(terms, lax.rem(me - of_core * (size // 2) - i + size, size), 1, 0)
            for i in range(size // 2)
        ]
        return jnp.concatenate(slabs, axis=0).reshape(half, blocks, LANES)

    kernel_grad = call(
        functools.partial(kernel_grad_body, size),
        shaped((2, half, positions), BF),
        [pltpu.VMEM((half * (blocks + PAD), LANES), F32)],
        place, halves(core), lax.ppermute(halves(1 - core), "core", SWAP),
        smem=1, micros=3,
    )
    (input_grad,) = chunked(
        final_body, 6, (wpv,), (gates, own),
        (pltpu.HBM((channels, positions), BF),), (back,), (turn_items,),
    )
    return input_grad.reshape(1, channels, positions), kernel_grad


def solution(mesh):
    sequences, groups = mesh.devices.shape
    size = round(groups ** (1 / 3))
    fine = Mesh(
        mesh.devices.reshape(2, sequences // 2, size, size, size), ("zl", "core") + RING
    )
    dp = ("zl", "core")
    signal = P(dp, None, SEQ)
    return jax.shard_map(
        per_device,
        mesh=fine,
        in_specs=(signal, P(None, None, SEQ), P(), P(), P(), signal),
        out_specs=(signal, P(None, dp, SEQ)),
        check_vma=False,
    )
```
